32 devices in a mesh: band: 2 (over x), lon: 16 (over z, y, core).
Axes of the slice: x: 2, y: 2, z: 4, core: 2. Of those that a mesh axis runs over, the one named last changes fastest.
Arguments:
- field: float32 [32, 90, 2048], P('band', None, 'lon'), parts along dimension 0, may hold values from -80 to 80
Outputs:
- coherence: float32 [2, 180, 90, 2048], P(None, 'band', None, 'lon'), parts along dimension 1
The draws below stay inside these ranges and needn't reach their ends.
There are 2 independent parts, one for each index of `band`. The reference program is written for one: setup_inputs(seed, part) draws one part's arguments, and reference() takes and returns one part's arrays. A program takes and returns all parts, laid end to end along the dimension named above; each array names one. Nothing has to cross between parts.
All inputs are finite; a program needn't handle non-finite values.
Results may differ from the reference program's by a relative error of at most 0.0002.
Values sent between devices are 32-bit elements; how exact they have to be, the bound alone decides.
No kernel may reach another device: no remote copies, remote signals or barrier semaphores. Data moves between devices by JAX's collectives and lax.ppermute only.
A program may use at most 128 MiB of HBM per device.

```python
import math
import jax
import jax.numpy as jnp
from jax import lax

LEV = 90
ROWS = 16
NLON = 2048


def draw_field(key, part):
    key_level, key_base = jax.random.split(key, 2)
    level_scale = jnp.exp(jax.random.uniform(key_level, (1, LEV, 1), jnp.float32, 0.0, math.log(10.0)))
    values = jnp.clip(jax.random.normal(key_base, (ROWS, LEV, NLON), jnp.float32), -6.0, 6.0) * level_scale
    return values.astype(jnp.float32)


def setup_inputs(seed: int = 0, part: int = 0) -> dict:
    keys = jax.random.split(jax.random.key(seed), 2)
    part_keys = jax.random.split(jax.random.fold_in(keys[1], part), 2)
    return {
        "field": draw_field(jax.random.fold_in(jax.random.fold_in(keys[1], part), 71), part),
    }


EPS = 1e-06

def coherence_block(block):
    real_part = block[0]
    imag_part = block[1]
    highest = lax.Precision.HIGHEST
    count = real_part.shape[0]
    cross_re = (jnp.einsum('rak,rbk->abk', real_part, real_part, precision=highest) + jnp.einsum('rak,rbk->abk', imag_part, imag_part, precision=highest)) / count
    cross_im = (jnp.einsum('rak,rbk->abk', imag_part, real_part, precision=highest) - jnp.einsum('rak,rbk->abk', real_part, imag_part, precision=highest)) / count
    power = lax.optimization_barrier(jnp.sum(real_part * real_part + imag_part * imag_part, axis=0)) / count
    scale = lax.rsqrt(power + EPS)
    factor = scale[:, None, :] * scale[None, :, :]
    return jnp.stack([cross_re * factor, cross_im * factor])

def reference(field):
    spectrum = jnp.fft.fft(field, axis=2)
    spec_re = jnp.real(spectrum).astype(jnp.float32)
    spec_im = jnp.imag(spectrum).astype(jnp.float32)
    stacked = jnp.stack([spec_re, spec_im])
    width = 1024 if NLON % 1024 == 0 else NLON
    count = NLON // width
    blocks = jnp.moveaxis(stacked.reshape(2, ROWS, LEV, count, width), 3, 0)
    result = lax.map(coherence_block, blocks)
    return jnp.moveaxis(result, 0, 3).reshape(2, LEV, LEV, NLON)
```

```python
import functools
import math

import jax
import jax.numpy as jnp
import numpy as np
from jax import lax
from jax.experimental import pallas as pl
from jax.experimental.pallas import tpu as pltpu
from jax.sharding import PartitionSpec as P

EPS = 1e-06
LANES = 128
TILE = 8


def wave_table(local_len, devices):
    lane = np.arange(local_len)
    low, p = lane // devices, lane % devices
    a = (local_len // devices) * p + low
    phase = (a[:, None] * np.arange(local_len)[None, :]) % local_len
    angle = -2.0 * np.pi * phase / local_len
    return np.concatenate([np.cos(angle), np.sin(angle)], axis=1).astype(np.float32)


def twiddle_table(local_len, devices):
    total = local_len * devices
    phase = (np.arange(devices)[:, None] * np.arange(local_len)[None, :]) % total
    angle = -2.0 * np.pi * phase / total
    return np.stack([np.cos(angle), np.sin(angle)]).astype(np.float32)


def swap_lanes(values):
    values = list(values)
    count = len(values)
    lane = lax.broadcasted_iota(jnp.int32, values[0].shape, 1)
    step = 1
    while step < count:
        clear = (lane & step) == 0
        for low in range(count):
            if low & step:
                continue
            first, second = values[low], values[low | step]
            values[low] = jnp.where(clear, first, pltpu.roll(second, step, 1))
            values[low | step] = jnp.where(clear, pltpu.roll(first, LANES - step, 1), second)
        step *= 2
    return values


def small_dft(values):
    count = len(values)
    if count == 1:
        return values
    even, odd = small_dft(values[0::2]), small_dft(values[1::2])
    lower, upper = [], []
    for d in range(count // 2):
        re, im = odd[d]
        if d == 0:
            pass
        elif 4 * d == count:
            re, im = im, -re
        elif 8 * d == count:
            root = math.sqrt(0.5)
            re, im = (re + im) * root, (im - re) * root
        elif 8 * d == 3 * count:
            root = math.sqrt(0.5)
            re, im = (im - re) * root, -(re + im) * root
        else:
            angle = -2.0 * math.pi * d / count
            cosine, sine = math.cos(angle), math.sin(angle)
            re, im = re * cosine - im * sine, re * sine + im * cosine
        lower.append((even[d][0] + re, even[d][1] + im))
        upper.append((even[d][0] - re, even[d][1] - im))
    return lower + upper


def transform_kernel(devices, block, x_ref, wave_ref, twiddle_ref, out_ref, mixed, product):
    for row in range(0, block, TILE):
        swapped = swap_lanes([x_ref[p, pl.ds(row, TILE), :] for p in range(devices)])
        for b in range(devices):
            mixed[pl.ds(b * block + row, TILE), :] = swapped[b]
    product[...] = jnp.dot(
        mixed[...], wave_ref[...], precision=lax.Precision.HIGHEST, preferred_element_type=jnp.float32
    )
    for row in range(0, block, TILE):
        values = []
        for b in range(devices):
            re = product[pl.ds(b * block + row, TILE), pl.ds(0, LANES)]
            im = product[pl.ds(b * block + row, TILE), pl.ds(LANES, LANES)]
            if b:
                cosine, sine = twiddle_ref[0, pl.ds(b, 1), :], twiddle_ref[1, pl.ds(b, 1), :]
                re, im = re * cosine - im * sine, re * sine + im * cosine
            values.append((re, im))
        for d, (re, im) in enumerate(small_dft(values)):
            out_ref[d, 0, pl.ds(row, TILE), :] = re
            out_ref[d, 1, pl.ds(row, TILE), :] = im


def transform(gathered):
    devices, levels, local_len = gathered.shape
    block = min(32, -(-levels // TILE) * TILE)
    steps = -(-levels // block)
    wave = jnp.asarray(wave_table(local_len, devices))
    twiddle = jnp.asarray(twiddle_table(local_len, devices))
    return pl.pallas_call(
        functools.partial(transform_kernel, devices, block),
        grid=(steps,),
        out_shape=jax.ShapeDtypeStruct((devices, 2, levels, local_len), jnp.float32),
        in_specs=[
            pl.BlockSpec((devices, block, local_len), lambda i: (0, i, 0)),
            pl.BlockSpec(wave.shape, lambda i: (0, 0)),
            pl.BlockSpec(twiddle.shape, lambda i: (0, 0, 0)),
        ],
        out_specs=pl.BlockSpec((devices, 2, block, local_len), lambda i: (0, 0, i, 0)),
        scratch_shapes=[
            pltpu.VMEM((devices * block, local_len), jnp.float32),
            pltpu.VMEM((devices * block, 2 * local_len), jnp.float32),
        ],
        compiler_params=pltpu.CompilerParams(vmem_limit_bytes=24 << 20),
        name="transform",
    )(gathered, wave, twiddle)


GROUP = 4
PAIR = 2


def coherence_kernel(rows, levels, tiles, padded, spec_ref, out_ref, norm, cross, sems):
    zero = jnp.zeros((TILE, LANES), jnp.float32)

    def normalise(level, size):
        res = [spec_ref[r, 0, pl.ds(level, size), :] for r in range(rows)]
        ims = [spec_ref[r, 1, pl.ds(level, size), :] for r in range(rows)]
        power = res[0] * res[0] + ims[0] * ims[0]
        for r in range(1, rows):
            power = power + (res[r] * res[r] + ims[r] * ims[r])
        scale = lax.rsqrt(power / rows + EPS) * (1.0 / math.sqrt(rows))
        for r in range(rows):
            re, im = res[r] * scale, ims[r] * scale
            norm[0, r, pl.ds(level, size), :] = re
            norm[1, r, pl.ds(level, size), :] = im
            norm[2, r, pl.ds(level, size), :] = re + im
            norm[3, r, pl.ds(level, size), :] = re - im

    whole = levels // TILE
    for level in range(whole * TILE, padded, TILE):
        for q in range(4):
            for r in range(rows):
                norm[q, r, pl.ds(level, TILE), :] = zero

    @pl.loop(0, whole)
    def _(tile):
        normalise(pl.multiple_of(tile * TILE, TILE), TILE)

    if levels % TILE:
        normalise(whole * TILE, levels % TILE)

    def products(a0, t0):
        sums = [[[None] * 3 for _ in range(PAIR)] for _ in range(GROUP)]
        for r in range(rows):
            right = [
                [norm[q, r, pl.ds(pl.multiple_of((t0 + t) * TILE, TILE), TILE), :] for q in (0, 2, 3)]
                for t in range(PAIR)
            ]
            for g in range(GROUP):
                left = [norm[q, r, pl.ds(a0 + g, TILE, stride=0), :] for q in (2, 0, 1)]
                for t in range(PAIR):
                    for i in range(3):
                        term = left[i] * right[t][i]
                        sums[g][t][i] = term if r == 0 else sums[g][t][i] + term
        for g in range(GROUP):
            for t in range(PAIR):
                one, two, three = sums[g][t]
                re, im = one - three, one - two
                level = pl.multiple_of((t0 + t) * TILE, TILE)
                straight = pl.multiple_of((a0 + g) * padded + level, TILE)
                mirrored = pl.ds(level * padded + a0 + g, TILE, stride=padded)
                cross[0, pl.ds(straight, TILE), :] = re
                cross[1, pl.ds(straight, TILE), :] = im
                cross[0, mirrored, :] = re
                cross[1, mirrored, :] = -im

    def copy(tile, count):
        planes = cross.reshape(2, padded, padded, LANES)
        return [
            pltpu.make_async_copy(
                planes.at[c, pl.ds(tile * TILE, count), pl.ds(0, levels), :],
                out_ref.at[c, pl.ds(tile * TILE, count)],
                sems.at[tile, c],
            )
            for c in range(2)
        ]

    def work(tile):
        @pl.loop(0, TILE // GROUP)
        def _(group):
            @pl.loop(0, (tiles - tile + PAIR - 1) // PAIR)
            def _(pair):
                products(tile * TILE + group * GROUP, tile + pair * PAIR)

    @pl.loop(0, whole)
    def _(tile):
        work(tile)
        for one in copy(tile, TILE):
            one.start()

    if levels % TILE:
        work(whole)
        for one in copy(whole, levels % TILE):
            one.start()

    @pl.loop(0, whole)
    def _(tile):
        for one in copy(tile, TILE):
            one.wait()

    if levels % TILE:
        for one in copy(whole, levels % TILE):
            one.wait()


def coherence(spectra):
    rows, _, levels, local_len = spectra.shape
    tiles = -(-levels // TILE)
    padded = (tiles + PAIR - 1) * TILE
    return pl.pallas_call(
        functools.partial(coherence_kernel, rows, levels, tiles, padded),
        out_shape=jax.ShapeDtypeStruct((2, levels, levels, local_len), jnp.float32),
        in_specs=[pl.BlockSpec(memory_space=pltpu.VMEM)],
        out_specs=pl.BlockSpec(memory_space=pl.ANY),
        scratch_shapes=[
            pltpu.VMEM((4, rows, padded, local_len), jnp.float32),
            pltpu.VMEM((2, padded * padded, local_len), jnp.float32),
            pltpu.SemaphoreType.DMA((tiles, 2)),
        ],
        compiler_params=pltpu.CompilerParams(vmem_limit_bytes=40 << 20),
        name="coherence",
    )(spectra)


def local(field):
    devices = lax.axis_size("lon")
    rows, levels, local_len = field.shape
    chunks = devices // rows
    size = -(-levels // chunks)
    outgoing = field
    if chunks > 1:
        outgoing = jnp.pad(field, ((0, 0), (0, chunks * size - levels), (0, 0)))
        outgoing = outgoing.reshape(devices, size, local_len)
    gathered = lax.all_to_all(outgoing, "lon", split_axis=0, concat_axis=0, tiled=True)
    blocks = transform(gathered)
    spectra = lax.all_to_all(blocks, "lon", split_axis=0, concat_axis=0, tiled=True)
    if chunks > 1:
        spectra = spectra.reshape(rows, chunks, 2, size, local_len).transpose(0, 2, 1, 3, 4)
        spectra = spectra.reshape(rows, 2, chunks * size, local_len)[:, :, :levels]
    return coherence(spectra)


def solution(mesh):
    in_specs = (P("band", None, "lon"),)
    out_specs = P(None, "band", None, "lon")
    return jax.shard_map(local, mesh=mesh, in_specs=in_specs, out_specs=out_specs, check_vma=False)
```

```python
import functools
import math

import jax
import jax.numpy as jnp
import numpy as np
from jax import lax
from jax.experimental import pallas as pl
from jax.experimental.pallas import tpu as pltpu
from jax.sharding import PartitionSpec as P

EPS = 1e-06
LANES = 128
TILE = 8


def wave_table(local_len, devices):
    lane = np.arange(local_len)
    low, p = lane // devices, lane % devices
    a = (local_len // devices) * p + low
    phase = (a[:, None] * np.arange(local_len)[None, :]) % local_len
    angle = -2.0 * np.pi * phase / local_len
    return np.concatenate([np.cos(angle), np.sin(angle)], axis=1).astype(np.float32)


def twiddle_table(local_len, devices):
    total = local_len * devices
    phase = (np.arange(devices)[:, None] * np.arange(local_len)[None, :]) % total
    angle = -2.0 * np.pi * phase / total
    return np.stack([np.cos(angle), np.sin(angle)]).astype(np.float32)


def swap_lanes(values):
    values = list(values)
    count = len(values)
    lane = lax.broadcasted_iota(jnp.int32, values[0].shape, 1)
    step = 1
    while step < count:
        clear = (lane & step) == 0
        for low in range(count):
            if low & step:
                continue
            first, second = values[low], values[low | step]
            values[low] = jnp.where(clear, first, pltpu.roll(second, step, 1))
            values[low | step] = jnp.where(clear, pltpu.roll(first, LANES - step, 1), second)
        step *= 2
    return values


def small_dft(values):
    count = len(values)
    if count == 1:
        return values
    even, odd = small_dft(values[0::2]), small_dft(values[1::2])
    lower, upper = [], []
    for d in range(count // 2):
        re, im = odd[d]
        if d == 0:
            pass
        elif 4 * d == count:
            re, im = im, -re
        elif 8 * d == count:
            root = math.sqrt(0.5)
            re, im = (re + im) * root, (im - re) * root
        elif 8 * d == 3 * count:
            root = math.sqrt(0.5)
            re, im = (im - re) * root, -(re + im) * root
        else:
            angle = -2.0 * math.pi * d / count
            cosine, sine = math.cos(angle), math.sin(angle)
            re, im = re * cosine - im * sine, re * sine + im * cosine
        lower.append((even[d][0] + re, even[d][1] + im))
        upper.append((even[d][0] - re, even[d][1] - im))
    return lower + upper


def transform_kernel(devices, lines, x_ref, wave_ref, twiddle_ref, out_ref, mixed, product):
    tiles = -(-lines // TILE)
    padded = tiles * TILE
    bases = [min(tile * TILE, lines - TILE) for tile in range(tiles)]
    for tile, base in enumerate(bases):
        swapped = swap_lanes([x_ref[pl.ds(p * lines + base, TILE), :] for p in range(devices)])
        for b in range(devices):
            mixed[pl.ds(b * padded + tile * TILE, TILE), :] = swapped[b]
    product[...] = jnp.dot(
        mixed[...], wave_ref[...], precision=lax.Precision.HIGHEST, preferred_element_type=jnp.float32
    )
    for tile, base in enumerate(bases):
        values = []
        for b in range(devices):
            row = b * padded + tile * TILE
            re = product[pl.ds(row, TILE), pl.ds(0, LANES)]
            im = product[pl.ds(row, TILE), pl.ds(LANES, LANES)]
            if b:
                cosine, sine = twiddle_ref[0, pl.ds(b, 1), :], twiddle_ref[1, pl.ds(b, 1), :]
                re, im = re * cosine - im * sine, re * sine + im * cosine
            values.append((re, im))
        for d, value in enumerate(small_dft(values)):
            for c in range(2):
                out_ref[pl.ds(2 * (d * lines + base) + c, TILE, stride=2), :] = value[c]


def transform(gathered, devices):
    total, local_len = gathered.shape
    lines = total // devices
    padded = -(-lines // TILE) * TILE
    wave = jnp.asarray(wave_table(local_len, devices))
    twiddle = jnp.asarray(twiddle_table(local_len, devices))
    return pl.pallas_call(
        functools.partial(transform_kernel, devices, lines),
        out_shape=jax.ShapeDtypeStruct((2 * total, local_len), jnp.float32),
        in_specs=[pl.BlockSpec(memory_space=pltpu.VMEM)] * 3,
        out_specs=pl.BlockSpec(memory_space=pltpu.VMEM),
        scratch_shapes=[
            pltpu.VMEM((devices * padded, local_len), jnp.float32),
            pltpu.VMEM((devices * padded, 2 * local_len), jnp.float32),
        ],
        compiler_params=pltpu.CompilerParams(vmem_limit_bytes=24 << 20),
        name="transform",
    )(gathered, wave, twiddle)


GROUP = 4
PAIR = 2


def coherence_kernel(rows, levels, spec_ref, out_ref, norm, cross, sems):
    tiles = -(-levels // TILE)

    def base(tile):
        return jnp.minimum(tile * TILE, levels - TILE)

    @pl.loop(0, tiles)
    def _(tile):
        def load(r, c):
            return spec_ref[pl.ds(2 * (base(tile) * rows + r) + c, TILE, stride=2 * rows), :]

        res = [load(r, 0) for r in range(rows)]
        ims = [load(r, 1) for r in range(rows)]
        power = res[0] * res[0] + ims[0] * ims[0]
        for r in range(1, rows):
            power = power + (res[r] * res[r] + ims[r] * ims[r])
        scale = lax.rsqrt(power / rows + EPS) * (1.0 / math.sqrt(rows))
        slot = pl.ds(pl.multiple_of(tile * TILE, TILE), TILE)
        for r in range(rows):
            re, im = res[r] * scale, ims[r] * scale
            norm[0, r, slot, :] = re
            norm[1, r, slot, :] = im
            norm[2, r, slot, :] = re + im
            norm[3, r, slot, :] = re - im

    def products(level, slot, pair):
        sums = [[[None] * 3 for _ in range(PAIR)] for _ in range(GROUP)]
        for r in range(rows):
            right = [
                [norm[q, r, pl.ds(pl.multiple_of(t * TILE, TILE), TILE), :] for q in (0, 2, 3)] for t in pair
            ]
            for g in range(GROUP):
                left = [norm[q, r, pl.ds(slot + g, TILE, stride=0), :] for q in (2, 0, 1)]
                for t in range(PAIR):
                    for i in range(3):
                        term = left[i] * right[t][i]
                        sums[g][t][i] = term if r == 0 else sums[g][t][i] + term
        for g in range(GROUP):
            for t in range(PAIR):
                one, two, three = sums[g][t]
                re, im = one - three, one - two
                a, b = level + g, base(pair[t])
                for c, straight, mirrored in ((0, re, re), (1, im, -im)):
                    cross[pl.ds(2 * (a * levels + b) + c, TILE, stride=2), :] = straight
                    cross[pl.ds(2 * (b * levels + a) + c, TILE, stride=2 * levels), :] = mirrored

    def work(tile, level, slot, groups):
        @pl.loop(0, groups)
        def _(group):
            @pl.loop(0, (tiles - tile + PAIR - 1) // PAIR)
            def _(step):
                first = tile + step * PAIR
                pair = [jnp.minimum(first + t, tiles - 1) for t in range(PAIR)]
                products(level + group * GROUP, slot + group * GROUP, pair)

    def copy(tile, count):
        part = pl.ds(pl.multiple_of(tile * (TILE * 2 * levels), TILE), count * 2 * levels)
        return pltpu.make_async_copy(cross.at[part], out_ref.at[part], sems.at[tile])

    last = tiles - 2

    @pl.loop(0, last)
    def _(tile):
        work(tile, tile * TILE, tile * TILE, TILE // GROUP)
        copy(tile, TILE).start()

    work(last, last * TILE, last * TILE, TILE // GROUP)
    rest = levels - (tiles - 1) * TILE
    groups = -(-rest // GROUP)
    work(tiles - 1, levels - groups * GROUP, tiles * TILE - groups * GROUP, groups)
    copy(last, levels - last * TILE).start()

    @pl.loop(0, last)
    def _(tile):
        copy(tile, TILE).wait()

    copy(last, levels - last * TILE).wait()


def coherence(spectra, rows, levels):
    local_len = spectra.shape[1]
    tiles = -(-levels // TILE)
    out_rows = 2 * levels * levels
    return pl.pallas_call(
        functools.partial(coherence_kernel, rows, levels),
        out_shape=jax.ShapeDtypeStruct((out_rows, local_len), jnp.float32),
        in_specs=[pl.BlockSpec(memory_space=pltpu.VMEM)],
        out_specs=pl.BlockSpec(memory_space=pl.ANY),
        scratch_shapes=[
            pltpu.VMEM((4, rows, tiles * TILE, local_len), jnp.float32),
            pltpu.VMEM((out_rows, local_len), jnp.float32),
            pltpu.SemaphoreType.DMA((tiles,)),
        ],
        compiler_params=pltpu.CompilerParams(vmem_limit_bytes=40 << 20),
        name="coherence",
    )(spectra)


def exchange(value, devices):
    rows, local_len = value.shape
    value = value.reshape(devices, rows // (2 * devices), 2, local_len)
    return lax.all_to_all(value, "lon", split_axis=0, concat_axis=0, tiled=True).reshape(rows, local_len)


def local(field):
    devices = lax.axis_size("lon")
    rows, levels, local_len = field.shape
    total = rows * levels
    share = -(-total // (2 * devices)) * 2
    lines = field.transpose(1, 0, 2).reshape(total, local_len)
    lines = jnp.pad(lines, ((0, share * devices - total), (0, 0)))
    spectra = exchange(transform(exchange(lines, devices), devices), devices)
    result = coherence(spectra, rows, levels)
    return result.reshape(levels, levels, 2, local_len).transpose(2, 0, 1, 3)


def solution(mesh):
    in_specs = (P("band", None, "lon"),)
    out_specs = P(None, "band", None, "lon")
    return jax.shard_map(local, mesh=mesh, in_specs=in_specs, out_specs=out_specs, check_vma=False)
```

```python
import functools
import math

import jax
import jax.numpy as jnp
import numpy as np
from jax import lax
from jax.experimental import pallas as pl
from jax.experimental.pallas import tpu as pltpu
from jax.sharding import PartitionSpec as P

EPS = 1e-06
LANES = 128
TILE = 8


def wave_table(local_len, devices):
    lane = np.arange(local_len)
    low, p = lane // devices, lane % devices
    a = (local_len // devices) * p + low
    phase = (a[:, None] * np.arange(local_len)[None, :]) % local_len
    angle = -2.0 * np.pi * phase / local_len
    return np.concatenate([np.cos(angle), np.sin(angle)], axis=1).astype(np.float32)


def twiddle_table(local_len, devices):
    total = local_len * devices
    phase = (np.arange(devices)[:, None] * np.arange(local_len)[None, :]) % total
    angle = -2.0 * np.pi * phase / total
    return np.stack([np.cos(angle), np.sin(angle)]).astype(np.float32)


def swap_lanes(values):
    values = list(values)
    count = len(values)
    lane = lax.broadcasted_iota(jnp.int32, values[0].shape, 1)
    step = 1
    while step < count:
        clear = (lane & step) == 0
        for low in range(count):
            if low & step:
                continue
            first, second = values[low], values[low | step]
            values[low] = jnp.where(clear, first, pltpu.roll(second, step, 1))
            values[low | step] = jnp.where(clear, pltpu.roll(first, LANES - step, 1), second)
        step *= 2
    return values


def small_dft(values):
    count = len(values)
    if count == 1:
        return values
    even, odd = small_dft(values[0::2]), small_dft(values[1::2])
    lower, upper = [], []
    for d in range(count // 2):
        re, im = odd[d]
        if d == 0:
            pass
        elif 4 * d == count:
            re, im = im, -re
        elif 8 * d == count:
            root = math.sqrt(0.5)
            re, im = (re + im) * root, (im - re) * root
        elif 8 * d == 3 * count:
            root = math.sqrt(0.5)
            re, im = (im - re) * root, -(re + im) * root
        else:
            angle = -2.0 * math.pi * d / count
            cosine, sine = math.cos(angle), math.sin(angle)
            re, im = re * cosine - im * sine, re * sine + im * cosine
        lower.append((even[d][0] + re, even[d][1] + im))
        upper.append((even[d][0] - re, even[d][1] - im))
    return lower + upper


def transform_kernel(devices, lines, x_ref, wave_ref, twiddle_ref, out_ref, mixed, product):
    tiles = -(-lines // TILE)
    padded = tiles * TILE
    bases = [min(tile * TILE, lines - TILE) for tile in range(tiles)]
    for tile, base in enumerate(bases):
        swapped = swap_lanes([x_ref[pl.ds(p * lines + base, TILE), :] for p in range(devices)])
        for b in range(devices):
            mixed[pl.ds(b * padded + tile * TILE, TILE), :] = swapped[b]
    product[...] = jnp.dot(
        mixed[...], wave_ref[...], precision=lax.Precision.HIGHEST, preferred_element_type=jnp.float32
    )
    for tile, base in enumerate(bases):
        values = []
        for b in range(devices):
            row = b * padded + tile * TILE
            re = product[pl.ds(row, TILE), pl.ds(0, LANES)]
            im = product[pl.ds(row, TILE), pl.ds(LANES, LANES)]
            if b:
                cosine, sine = twiddle_ref[0, pl.ds(b, 1), :], twiddle_ref[1, pl.ds(b, 1), :]
                re, im = re * cosine - im * sine, re * sine + im * cosine
            values.append((re, im))
        for d, value in enumerate(small_dft(values)):
            for c in range(2):
                out_ref[pl.ds(2 * (d * lines + base) + c, TILE, stride=2), :] = value[c]


def transform(gathered, devices):
    total, local_len = gathered.shape
    lines = total // devices
    padded = -(-lines // TILE) * TILE
    wave = jnp.asarray(wave_table(local_len, devices))
    twiddle = jnp.asarray(twiddle_table(local_len, devices))
    return pl.pallas_call(
        functools.partial(transform_kernel, devices, lines),
        out_shape=jax.ShapeDtypeStruct((2 * total, local_len), jnp.float32),
        in_specs=[pl.BlockSpec(memory_space=pltpu.VMEM)] * 3,
        out_specs=pl.BlockSpec(memory_space=pltpu.VMEM),
        scratch_shapes=[
            pltpu.VMEM((devices * padded, local_len), jnp.float32),
            pltpu.VMEM((devices * padded, 2 * local_len), jnp.float32),
        ],
        cost_estimate=pl.CostEstimate(
            flops=2 * total * 2 * local_len * local_len, bytes_accessed=12 * total * local_len, transcendentals=0
        ),
        compiler_params=pltpu.CompilerParams(vmem_limit_bytes=24 << 20),
        name="transform",
    )(gathered, wave, twiddle)


GROUP = 4
PAIR = 2
QUANTITIES = 4


def normalise(rows, levels, spec_ref, norm):
    @pl.loop(0, -(-levels // TILE))
    def _(tile):
        first = jnp.minimum(tile * TILE, levels - TILE)

        def load(r, c):
            return spec_ref[pl.ds(2 * (first * rows + r) + c, TILE, stride=2 * rows), :]

        res = [load(r, 0) for r in range(rows)]
        ims = [load(r, 1) for r in range(rows)]
        power = res[0] * res[0] + ims[0] * ims[0]
        for r in range(1, rows):
            power = power + (res[r] * res[r] + ims[r] * ims[r])
        scale = lax.rsqrt(power / rows + EPS) * (1.0 / math.sqrt(rows))
        slot = pl.ds(pl.multiple_of(tile * TILE, TILE), TILE)
        for r in range(rows):
            re, im = res[r] * scale, ims[r] * scale
            norm[0, r, slot, :] = re
            norm[1, r, slot, :] = im
            norm[2, r, slot, :] = re + im
            norm[3, r, slot, :] = re - im


def products(rows, stride, left_norm, right_norm, level, slot, pair, cross):
    sums = [[[None] * 3 for _ in pair] for _ in range(GROUP)]
    for r in range(rows):
        right = [
            [right_norm[q, r, pl.ds(pl.multiple_of(t * TILE, TILE), TILE), :] for q in (0, 2, 3)] for t, _ in pair
        ]
        for g in range(GROUP):
            left = [left_norm[q, r, pl.ds(slot + g, TILE, stride=0), :] for q in (2, 0, 1)]
            for t in range(len(pair)):
                for i in range(3):
                    term = left[i] * right[t][i]
                    sums[g][t][i] = term if r == 0 else sums[g][t][i] + term
    for g in range(GROUP):
        for t, (_, b) in enumerate(pair):
            one, two, three = sums[g][t]
            re, im = one - three, one - two
            a = level + g
            for c, straight, mirrored in ((0, re, re), (1, im, -im)):
                cross[pl.ds(2 * (a * stride + b) + c, TILE, stride=2), :] = straight
                cross[pl.ds(2 * (b * stride + a) + c, TILE, stride=2 * stride), :] = mirrored


def sweep(rows, stride, left, right, groups, level, slot, tile, cross):
    right_norm, levels, offset = right
    tiles = -(-levels // TILE)

    @pl.loop(0, groups)
    def _(group):
        @pl.loop(0, (tiles - tile + PAIR - 1) // PAIR)
        def _(step):
            pair = []
            for t in range(PAIR):
                index = jnp.minimum(tile + step * PAIR + t, tiles - 1)
                pair.append((index, offset + jnp.minimum(index * TILE, levels - TILE)))
            products(rows, stride, left, right_norm, level + group * GROUP, slot + group * GROUP, pair, cross)


def first_kernel(rows, levels, spec_ref, norm, cross):
    normalise(rows, levels, spec_ref, norm)

    @pl.loop(0, levels // TILE)
    def _(tile):
        sweep(rows, levels, norm, (norm, levels, 0), TILE // GROUP, tile * TILE, tile * TILE, tile, cross)


def second_kernel(rows, known, levels, first_norm, inner_ref, spec_ref, out_ref, norm, cross, sems):
    total = known + levels
    normalise(rows, levels, spec_ref, norm)

    def copy(tile, count):
        part = pl.ds(pl.multiple_of(tile * (TILE * 2 * total), TILE), count * 2 * total)
        return pltpu.make_async_copy(cross.at[part], out_ref.at[part], sems.at[tile])

    whole = known // TILE

    @pl.loop(0, whole)
    def _(tile):
        @pl.loop(0, TILE)
        def _(i):
            level = tile * TILE + i
            for row in range(0, 2 * known, TILE):
                cross[pl.ds(2 * level * total + row, TILE), :] = inner_ref[pl.ds(2 * level * known + row, TILE), :]

        sweep(rows, total, first_norm, (norm, levels, known), TILE // GROUP, tile * TILE, tile * TILE, 0, cross)
        copy(tile, TILE).start()

    tiles = -(-levels // TILE)
    last = tiles - 2

    @pl.loop(0, last)
    def _(tile):
        sweep(rows, total, norm, (norm, levels, known), TILE // GROUP, known + tile * TILE, tile * TILE, tile, cross)
        copy(whole + tile, TILE).start()

    sweep(rows, total, norm, (norm, levels, known), TILE // GROUP, known + last * TILE, last * TILE, last, cross)
    groups = -(-(levels - (tiles - 1) * TILE) // GROUP)
    start, slot = total - groups * GROUP, tiles * TILE - groups * GROUP
    sweep(rows, total, norm, (norm, levels, known), groups, start, slot, tiles - 1, cross)
    copy(whole + last, levels - last * TILE).start()

    @pl.loop(0, whole + last)
    def _(tile):
        copy(tile, TILE).wait()

    copy(whole + last, levels - last * TILE).wait()


def cost(rows, pairs, nbytes):
    return pl.CostEstimate(flops=6 * rows * pairs * LANES, bytes_accessed=nbytes, transcendentals=0)


def first_coherence(spectra, rows, levels):
    local_len = spectra.shape[1]
    norm = jax.ShapeDtypeStruct((QUANTITIES, rows, -(-levels // TILE) * TILE, local_len), jnp.float32)
    inner = jax.ShapeDtypeStruct((2 * levels * levels, local_len), jnp.float32)
    return pl.pallas_call(
        functools.partial(first_kernel, rows, levels),
        out_shape=(norm, inner),
        in_specs=[pl.BlockSpec(memory_space=pltpu.VMEM)],
        out_specs=(pl.BlockSpec(memory_space=pltpu.VMEM),) * 2,
        cost_estimate=cost(rows, levels * levels // 2, 4 * (spectra.size + norm.size + inner.size)),
        compiler_params=pltpu.CompilerParams(vmem_limit_bytes=24 << 20),
        name="first_coherence",
    )(spectra)


def second_coherence(norm, inner, spectra, rows, known, levels):
    local_len = spectra.shape[1]
    total = known + levels
    tiles = -(-levels // TILE)
    out_rows = 2 * total * total
    return pl.pallas_call(
        functools.partial(second_kernel, rows, known, levels),
        out_shape=jax.ShapeDtypeStruct((out_rows, local_len), jnp.float32),
        in_specs=[pl.BlockSpec(memory_space=pltpu.VMEM)] * 3,
        out_specs=pl.BlockSpec(memory_space=pl.ANY),
        scratch_shapes=[
            pltpu.VMEM((QUANTITIES, rows, tiles * TILE, local_len), jnp.float32),
            pltpu.VMEM((out_rows, local_len), jnp.float32),
            pltpu.SemaphoreType.DMA((known // TILE + tiles,)),
        ],
        cost_estimate=cost(rows, (total * total - known * known) // 2, 4 * (norm.size + spectra.size + out_rows * local_len)),
        compiler_params=pltpu.CompilerParams(vmem_limit_bytes=40 << 20),
        name="second_coherence",
    )(norm, inner, spectra)


def exchange(value, devices):
    rows, local_len = value.shape
    value = value.reshape(devices, rows // (2 * devices), 2, local_len)
    return lax.all_to_all(value, "lon", split_axis=0, concat_axis=0, tiled=True).reshape(rows, local_len)


def local(field):
    devices = lax.axis_size("lon")
    rows, levels, local_len = field.shape
    known = (levels // 2 + TILE - 1) // TILE * TILE
    lines = field.transpose(1, 0, 2).reshape(rows * levels, local_len)
    gathered = []
    for piece in (lines[: known * rows], lines[known * rows :]):
        share = max(TILE, -(-piece.shape[0] // (2 * devices)) * 2)
        gathered.append(exchange(jnp.pad(piece, ((0, share * devices - piece.shape[0]), (0, 0))), devices))
    first, second = [exchange(transform(piece, devices), devices) for piece in gathered]
    norm, inner = first_coherence(first, rows, known)
    result = second_coherence(norm, inner, second, rows, known, levels - known)
    return result.reshape(levels, levels, 2, local_len).transpose(2, 0, 1, 3)


def solution(mesh):
    in_specs = (P("band", None, "lon"),)
    out_specs = P(None, "band", None, "lon")
    return jax.shard_map(local, mesh=mesh, in_specs=in_specs, out_specs=out_specs, check_vma=False)
```

```python
import functools
import math

import jax
import jax.numpy as jnp
import numpy as np
from jax import lax
from jax.experimental import pallas as pl
from jax.experimental.pallas import tpu as pltpu
from jax.sharding import PartitionSpec as P

EPS = 1e-06
LANES = 128
TILE = 8


def wave_table(local_len, devices):
    lane = np.arange(local_len)
    low, p = lane // devices, lane % devices
    a = (local_len // devices) * p + low
    phase = (a[:, None] * np.arange(local_len)[None, :]) % local_len
    angle = -2.0 * np.pi * phase / local_len
    return np.concatenate([np.cos(angle), np.sin(angle)], axis=1).astype(np.float32)


def twiddle_table(local_len, devices):
    total = local_len * devices
    phase = (np.arange(devices)[:, None] * np.arange(local_len)[None, :]) % total
    angle = -2.0 * np.pi * phase / total
    return np.stack([np.cos(angle), np.sin(angle)]).astype(np.float32)


def swap_lanes(values):
    values = list(values)
    count = len(values)
    lane = lax.broadcasted_iota(jnp.int32, values[0].shape, 1)
    step = 1
    while step < count:
        clear = (lane & step) == 0
        for low in range(count):
            if low & step:
                continue
            first, second = values[low], values[low | step]
            values[low] = jnp.where(clear, first, pltpu.roll(second, step, 1))
            values[low | step] = jnp.where(clear, pltpu.roll(first, LANES - step, 1), second)
        step *= 2
    return values


def small_dft(values):
    count = len(values)
    if count == 1:
        return values
    even, odd = small_dft(values[0::2]), small_dft(values[1::2])
    lower, upper = [], []
    for d in range(count // 2):
        re, im = odd[d]
        if d == 0:
            pass
        elif 4 * d == count:
            re, im = im, -re
        elif 8 * d == count:
            root = math.sqrt(0.5)
            re, im = (re + im) * root, (im - re) * root
        elif 8 * d == 3 * count:
            root = math.sqrt(0.5)
            re, im = (im - re) * root, -(re + im) * root
        else:
            angle = -2.0 * math.pi * d / count
            cosine, sine = math.cos(angle), math.sin(angle)
            re, im = re * cosine - im * sine, re * sine + im * cosine
        lower.append((even[d][0] + re, even[d][1] + im))
        upper.append((even[d][0] - re, even[d][1] - im))
    return lower + upper


def transform_kernel(devices, lines, x_ref, wave_ref, twiddle_ref, out_ref, mixed, product):
    tiles = -(-lines // TILE)
    padded = tiles * TILE
    bases = [min(tile * TILE, lines - TILE) for tile in range(tiles)]
    for tile, base in enumerate(bases):
        swapped = swap_lanes([x_ref[pl.ds(p * lines + base, TILE), :] for p in range(devices)])
        for b in range(devices):
            mixed[pl.ds(b * padded + tile * TILE, TILE), :] = swapped[b]
    product[...] = jnp.dot(
        mixed[...], wave_ref[...], precision=lax.Precision.HIGHEST, preferred_element_type=jnp.float32
    )
    for tile, base in enumerate(bases):
        values = []
        for b in range(devices):
            row = b * padded + tile * TILE
            re = product[pl.ds(row, TILE), pl.ds(0, LANES)]
            im = product[pl.ds(row, TILE), pl.ds(LANES, LANES)]
            if b:
                cosine, sine = twiddle_ref[0, pl.ds(b, 1), :], twiddle_ref[1, pl.ds(b, 1), :]
                re, im = re * cosine - im * sine, re * sine + im * cosine
            values.append((re, im))
        for d, value in enumerate(small_dft(values)):
            for c in range(2):
                out_ref[pl.ds(2 * (d * lines + base) + c, TILE, stride=2), :] = value[c]


def transform(gathered, devices):
    total, local_len = gathered.shape
    lines = total // devices
    padded = -(-lines // TILE) * TILE
    wave = jnp.asarray(wave_table(local_len, devices))
    twiddle = jnp.asarray(twiddle_table(local_len, devices))
    return pl.pallas_call(
        functools.partial(transform_kernel, devices, lines),
        out_shape=jax.ShapeDtypeStruct((2 * total, local_len), jnp.float32),
        in_specs=[pl.BlockSpec(memory_space=pltpu.VMEM)] * 3,
        out_specs=pl.BlockSpec(memory_space=pltpu.VMEM),
        scratch_shapes=[
            pltpu.VMEM((devices * padded, local_len), jnp.float32),
            pltpu.VMEM((devices * padded, 2 * local_len), jnp.float32),
        ],
        compiler_params=pltpu.CompilerParams(vmem_limit_bytes=24 << 20),
        name="transform",
    )(gathered, wave, twiddle)


GROUP = 4
PAIR = 2


def coherence_kernel(rows, levels, spec_ref, out_ref, norm, cross, sems):
    tiles = -(-levels // TILE)

    def base(tile):
        return jnp.minimum(tile * TILE, levels - TILE)

    @pl.loop(0, tiles)
    def _(tile):
        def load(r, c):
            return spec_ref[pl.ds(2 * (base(tile) * rows + r) + c, TILE, stride=2 * rows), :]

        res = [load(r, 0) for r in range(rows)]
        ims = [load(r, 1) for r in range(rows)]
        power = res[0] * res[0] + ims[0] * ims[0]
        for r in range(1, rows):
            power = power + (res[r] * res[r] + ims[r] * ims[r])
        scale = lax.rsqrt(power / rows + EPS) * (1.0 / math.sqrt(rows))
        slot = pl.ds(pl.multiple_of(tile * TILE, TILE), TILE)
        for r in range(rows):
            re, im = res[r] * scale, ims[r] * scale
            norm[0, r, slot, :] = re
            norm[1, r, slot, :] = im
            norm[2, r, slot, :] = re + im
            norm[3, r, slot, :] = re - im

    def products(level, slot, pair, group):
        sums = [[[None] * 3 for _ in pair] for _ in range(group)]
        for r in range(rows):
            right = [
                [norm[q, r, pl.ds(pl.multiple_of(t * TILE, TILE), TILE), :] for q in (0, 2, 3)] for t in pair
            ]
            for g in range(group):
                left = [norm[q, r, pl.ds(slot + g, TILE, stride=0), :] for q in (2, 0, 1)]
                for t in range(len(pair)):
                    for i in range(3):
                        term = left[i] * right[t][i]
                        sums[g][t][i] = term if r == 0 else sums[g][t][i] + term
        for g in range(group):
            for t in range(len(pair)):
                one, two, three = sums[g][t]
                re, im = one - three, one - two
                a, b = level + g, base(pair[t])
                for c, straight, mirrored in ((0, re, re), (1, im, -im)):
                    cross[pl.ds(2 * (a * levels + b) + c, TILE, stride=2), :] = straight
                    cross[pl.ds(2 * (b * levels + a) + c, TILE, stride=2 * levels), :] = mirrored

    def work(tile, level, slot, groups):
        count = tiles - tile

        @pl.loop(0, count // PAIR)
        def _(step):
            first = tile + step * PAIR
            for group in range(groups):
                products(level + group * GROUP, slot + group * GROUP, [first + t for t in range(PAIR)], GROUP)

        def rest():
            products(level, slot, [tiles - 1], groups * GROUP)

        if not isinstance(count, int):
            pl.when(count % PAIR == 1)(rest)
        elif count % PAIR:
            rest()

    def copy(tile, count):
        part = pl.ds(pl.multiple_of(tile * (TILE * 2 * levels), TILE), count * 2 * levels)
        return pltpu.make_async_copy(cross.at[part], out_ref.at[part], sems.at[tile])

    last = tiles - 2

    @pl.loop(0, last)
    def _(tile):
        work(tile, tile * TILE, tile * TILE, TILE // GROUP)
        copy(tile, TILE).start()

    work(last, last * TILE, last * TILE, TILE // GROUP)
    rest = levels - (tiles - 1) * TILE
    groups = -(-rest // GROUP)
    work(tiles - 1, levels - groups * GROUP, tiles * TILE - groups * GROUP, groups)
    copy(last, levels - last * TILE).start()

    @pl.loop(0, last)
    def _(tile):
        copy(tile, TILE).wait()

    copy(last, levels - last * TILE).wait()


def coherence(spectra, rows, levels):
    local_len = spectra.shape[1]
    tiles = -(-levels // TILE)
    out_rows = 2 * levels * levels
    return pl.pallas_call(
        functools.partial(coherence_kernel, rows, levels),
        out_shape=jax.ShapeDtypeStruct((out_rows, local_len), jnp.float32),
        in_specs=[pl.BlockSpec(memory_space=pltpu.VMEM)],
        out_specs=pl.BlockSpec(memory_space=pl.ANY),
        scratch_shapes=[
            pltpu.VMEM((4, rows, tiles * TILE, local_len), jnp.float32),
            pltpu.VMEM((out_rows, local_len), jnp.float32),
            pltpu.SemaphoreType.DMA((tiles,)),
        ],
        compiler_params=pltpu.CompilerParams(vmem_limit_bytes=40 << 20),
        name="coherence",
    )(spectra)


def exchange(value, devices):
    rows, local_len = value.shape
    value = value.reshape(devices, rows // (2 * devices), 2, local_len)
    return lax.all_to_all(value, "lon", split_axis=0, concat_axis=0, tiled=True).reshape(rows, local_len)


def local(field):
    devices = lax.axis_size("lon")
    rows, levels, local_len = field.shape
    total = rows * levels
    share = -(-total // (2 * devices)) * 2
    lines = field.transpose(1, 0, 2).reshape(total, local_len)
    lines = jnp.pad(lines, ((0, share * devices - total), (0, 0)))
    spectra = exchange(transform(exchange(lines, devices), devices), devices)
    result = coherence(spectra, rows, levels)
    return result.reshape(levels, levels, 2, local_len).transpose(2, 0, 1, 3)


def solution(mesh):
    in_specs = (P("band", None, "lon"),)
    out_specs = P(None, "band", None, "lon")
    return jax.shard_map(local, mesh=mesh, in_specs=in_specs, out_specs=out_specs, check_vma=False)
```

```python
import functools
import math

import jax
import jax.numpy as jnp
import numpy as np
from jax import lax
from jax.experimental import pallas as pl
from jax.experimental.pallas import tpu as pltpu
from jax.sharding import PartitionSpec as P

EPS = 1e-06
LANES = 128
TILE = 8


def wave_table(local_len, devices):
    lane = np.arange(local_len)
    low, p = lane // devices, lane % devices
    a = (local_len // devices) * p + low
    phase = (a[:, None] * np.arange(local_len)[None, :]) % local_len
    angle = -2.0 * np.pi * phase / local_len
    return np.concatenate([np.cos(angle), np.sin(angle)], axis=1).astype(np.float32)


def twiddle_table(local_len, devices):
    total = local_len * devices
    phase = (np.arange(devices)[:, None] * np.arange(local_len)[None, :]) % total
    angle = -2.0 * np.pi * phase / total
    return np.stack([np.cos(angle), np.sin(angle)]).astype(np.float32)


def swap_lanes(values):
    values = list(values)
    count = len(values)
    lane = lax.broadcasted_iota(jnp.int32, values[0].shape, 1)
    step = 1
    while step < count:
        clear = (lane & step) == 0
        for low in range(count):
            if low & step:
                continue
            first, second = values[low], values[low | step]
            values[low] = jnp.where(clear, first, pltpu.roll(second, step, 1))
            values[low | step] = jnp.where(clear, pltpu.roll(first, LANES - step, 1), second)
        step *= 2
    return values


def small_dft(values):
    count = len(values)
    if count == 1:
        return values
    even, odd = small_dft(values[0::2]), small_dft(values[1::2])
    lower, upper = [], []
    for d in range(count // 2):
        re, im = odd[d]
        if d == 0:
            pass
        elif 4 * d == count:
            re, im = im, -re
        elif 8 * d == count:
            root = math.sqrt(0.5)
            re, im = (re + im) * root, (im - re) * root
        elif 8 * d == 3 * count:
            root = math.sqrt(0.5)
            re, im = (im - re) * root, -(re + im) * root
        else:
            angle = -2.0 * math.pi * d / count
            cosine, sine = math.cos(angle), math.sin(angle)
            re, im = re * cosine - im * sine, re * sine + im * cosine
        lower.append((even[d][0] + re, even[d][1] + im))
        upper.append((even[d][0] - re, even[d][1] - im))
    return lower + upper


def transform_kernel(devices, lines, x_ref, wave_ref, twiddle_ref, out_ref, mixed, product):
    tiles = -(-lines // TILE)
    padded = tiles * TILE
    bases = [min(tile * TILE, lines - TILE) for tile in range(tiles)]
    for tile, base in enumerate(bases):
        swapped = swap_lanes([x_ref[pl.ds(p * lines + base, TILE), :] for p in range(devices)])
        for b in range(devices):
            mixed[pl.ds(b * padded + tile * TILE, TILE), :] = swapped[b]
    product[...] = jnp.dot(
        mixed[...], wave_ref[...], precision=lax.Precision.HIGHEST, preferred_element_type=jnp.float32
    )
    for tile, base in enumerate(bases):
        values = []
        for b in range(devices):
            row = b * padded + tile * TILE
            re = product[pl.ds(row, TILE), pl.ds(0, LANES)]
            im = product[pl.ds(row, TILE), pl.ds(LANES, LANES)]
            if b:
                cosine, sine = twiddle_ref[0, pl.ds(b, 1), :], twiddle_ref[1, pl.ds(b, 1), :]
                re, im = re * cosine - im * sine, re * sine + im * cosine
            values.append((re, im))
        for d, value in enumerate(small_dft(values)):
            for c in range(2):
                out_ref[pl.ds(2 * (d * lines + base) + c, TILE, stride=2), :] = value[c]


def transform(gathered, devices):
    total, local_len = gathered.shape
    lines = total // devices
    padded = -(-lines // TILE) * TILE
    wave = jnp.asarray(wave_table(local_len, devices))
    twiddle = jnp.asarray(twiddle_table(local_len, devices))
    return pl.pallas_call(
        functools.partial(transform_kernel, devices, lines),
        out_shape=jax.ShapeDtypeStruct((2 * total, local_len), jnp.float32),
        in_specs=[pl.BlockSpec(memory_space=pltpu.VMEM)] * 3,
        out_specs=pl.BlockSpec(memory_space=pltpu.VMEM),
        scratch_shapes=[
            pltpu.VMEM((devices * padded, local_len), jnp.float32),
            pltpu.VMEM((devices * padded, 2 * local_len), jnp.float32),
        ],
        compiler_params=pltpu.CompilerParams(vmem_limit_bytes=24 << 20),
        name="transform",
    )(gathered, wave, twiddle)


GROUP = 4
PAIR = 2


def coherence_kernel(rows, levels, spec_ref, out_ref, pitched, norm, cross, sems):
    tiles = -(-levels // TILE)

    def base(tile):
        return jnp.minimum(tile * TILE, levels - TILE)

    pitch = 2 * rows + 1
    for level in range(levels):
        for row in range(0, 2 * rows, TILE):
            pitched[pl.ds(level * pitch + row, TILE), :] = spec_ref[pl.ds(level * 2 * rows + row, TILE), :]

    @pl.loop(0, tiles)
    def _(tile):
        def load(r, c):
            return pitched[pl.ds(base(tile) * pitch + 2 * r + c, TILE, stride=pitch), :]

        res = [load(r, 0) for r in range(rows)]
        ims = [load(r, 1) for r in range(rows)]
        power = res[0] * res[0] + ims[0] * ims[0]
        for r in range(1, rows):
            power = power + (res[r] * res[r] + ims[r] * ims[r])
        scale = lax.rsqrt(power / rows + EPS) * (1.0 / math.sqrt(rows))
        slot = pl.ds(pl.multiple_of(tile * TILE, TILE), TILE)
        for r in range(rows):
            re, im = res[r] * scale, ims[r] * scale
            norm[0, r, slot, :] = re
            norm[1, r, slot, :] = im
            norm[2, r, slot, :] = re + im
            norm[3, r, slot, :] = re - im

    def products(level, slot, pair, group):
        sums = [[[None] * 3 for _ in pair] for _ in range(group)]
        for r in range(rows):
            right = [
                [norm[q, r, pl.ds(pl.multiple_of(t * TILE, TILE), TILE), :] for q in (0, 2, 3)] for t in pair
            ]
            for g in range(group):
                left = [norm[q, r, pl.ds(slot + g, TILE, stride=0), :] for q in (2, 0, 1)]
                for t in range(len(pair)):
                    for i in range(3):
                        term = left[i] * right[t][i]
                        sums[g][t][i] = term if r == 0 else sums[g][t][i] + term
        for g in range(group):
            for t in range(len(pair)):
                one, two, three = sums[g][t]
                re, im = one - three, one - two
                a, b = level + g, base(pair[t])
                for c, straight, mirrored in ((0, re, re), (1, im, -im)):
                    cross[pl.ds(2 * (a * levels + b) + c, TILE, stride=2), :] = straight
                    cross[pl.ds(2 * (b * levels + a) + c, TILE, stride=2 * levels), :] = mirrored

    def work(tile, level, slot, groups):
        count = tiles - tile
        steps = count // (2 * PAIR)
        left = count - steps * 2 * PAIR

        def pairs(first, number):
            for pair in range(number):
                for group in range(groups):
                    here = [first + pair * PAIR + t for t in range(PAIR)]
                    products(level + group * GROUP, slot + group * GROUP, here, GROUP)

        @pl.loop(0, steps)
        def _(step):
            pairs(tile + step * 2 * PAIR, 2)

        def end(number):
            pairs(tile + steps * 2 * PAIR, number // PAIR)
            if number % PAIR:
                products(level, slot, [tiles - 1], groups * GROUP)

        for number in range(1, 2 * PAIR):
            if not isinstance(count, int):
                pl.when(left == number)(functools.partial(end, number))
            elif left == number:
                end(number)

    def copy(tile, count):
        part = pl.ds(pl.multiple_of(tile * (TILE * 2 * levels), TILE), count * 2 * levels)
        return pltpu.make_async_copy(cross.at[part], out_ref.at[part], sems.at[tile])

    last = tiles - 2

    @pl.loop(0, last)
    def _(tile):
        work(tile, tile * TILE, tile * TILE, TILE // GROUP)
        copy(tile, TILE).start()

    work(last, last * TILE, last * TILE, TILE // GROUP)
    rest = levels - (tiles - 1) * TILE
    groups = -(-rest // GROUP)
    work(tiles - 1, levels - groups * GROUP, tiles * TILE - groups * GROUP, groups)
    copy(last, levels - last * TILE).start()

    @pl.loop(0, last)
    def _(tile):
        copy(tile, TILE).wait()

    copy(last, levels - last * TILE).wait()


def coherence(spectra, rows, levels):
    local_len = spectra.shape[1]
    tiles = -(-levels // TILE)
    out_rows = 2 * levels * levels
    return pl.pallas_call(
        functools.partial(coherence_kernel, rows, levels),
        out_shape=jax.ShapeDtypeStruct((out_rows, local_len), jnp.float32),
        in_specs=[pl.BlockSpec(memory_space=pltpu.VMEM)],
        out_specs=pl.BlockSpec(memory_space=pl.ANY),
        scratch_shapes=[
            pltpu.VMEM((levels * (2 * rows + 1), local_len), jnp.float32),
            pltpu.VMEM((4, rows, tiles * TILE, local_len), jnp.float32),
            pltpu.VMEM((out_rows, local_len), jnp.float32),
            pltpu.SemaphoreType.DMA((tiles,)),
        ],
        compiler_params=pltpu.CompilerParams(vmem_limit_bytes=40 << 20),
        name="coherence",
    )(spectra)


def exchange(value, devices):
    rows, local_len = value.shape
    value = value.reshape(devices, rows // (2 * devices), 2, local_len)
    return lax.all_to_all(value, "lon", split_axis=0, concat_axis=0, tiled=True).reshape(rows, local_len)


def local(field):
    devices = lax.axis_size("lon")
    rows, levels, local_len = field.shape
    total = rows * levels
    share = -(-total // (2 * devices)) * 2
    lines = field.transpose(1, 0, 2).reshape(total, local_len)
    lines = jnp.pad(lines, ((0, share * devices - total), (0, 0)))
    spectra = exchange(transform(exchange(lines, devices), devices), devices)
    result = coherence(spectra, rows, levels)
    return result.reshape(levels, levels, 2, local_len).transpose(2, 0, 1, 3)


def solution(mesh):
    in_specs = (P("band", None, "lon"),)
    out_specs = P(None, "band", None, "lon")
    return jax.shard_map(local, mesh=mesh, in_specs=in_specs, out_specs=out_specs, check_vma=False)
```

```python
import functools
import math

import jax
import jax.numpy as jnp
import numpy as np
from jax import lax
from jax.experimental import pallas as pl
from jax.experimental.pallas import tpu as pltpu
from jax.sharding import PartitionSpec as P

EPS = 1e-06
LANES = 128
TILE = 8


def wave_table(local_len, devices):
    lane = np.arange(local_len)
    low, p = lane // devices, lane % devices
    a = (local_len // devices) * p + low
    phase = (a[:, None] * np.arange(local_len)[None, :]) % local_len
    angle = -2.0 * np.pi * phase / local_len
    return np.concatenate([np.cos(angle), np.sin(angle)], axis=1).astype(np.float32)


def twiddle_table(local_len, devices):
    total = local_len * devices
    phase = (np.arange(devices)[:, None] * np.arange(local_len)[None, :]) % total
    angle = -2.0 * np.pi * phase / total
    return np.stack([np.cos(angle), np.sin(angle)]).astype(np.float32)


def swap_lanes(values):
    values = list(values)
    count = len(values)
    lane = lax.broadcasted_iota(jnp.int32, values[0].shape, 1)
    step = 1
    while step < count:
        clear = (lane & step) == 0
        for low in range(count):
            if low & step:
                continue
            first, second = values[low], values[low | step]
            values[low] = jnp.where(clear, first, pltpu.roll(second, step, 1))
            values[low | step] = jnp.where(clear, pltpu.roll(first, LANES - step, 1), second)
        step *= 2
    return values


def small_dft(values):
    count = len(values)
    if count == 1:
        return values
    even, odd = small_dft(values[0::2]), small_dft(values[1::2])
    lower, upper = [], []
    for d in range(count // 2):
        re, im = odd[d]
        if d == 0:
            pass
        elif 4 * d == count:
            re, im = im, -re
        elif 8 * d == count:
            root = math.sqrt(0.5)
            re, im = (re + im) * root, (im - re) * root
        elif 8 * d == 3 * count:
            root = math.sqrt(0.5)
            re, im = (im - re) * root, -(re + im) * root
        else:
            angle = -2.0 * math.pi * d / count
            cosine, sine = math.cos(angle), math.sin(angle)
            re, im = re * cosine - im * sine, re * sine + im * cosine
        lower.append((even[d][0] + re, even[d][1] + im))
        upper.append((even[d][0] - re, even[d][1] - im))
    return lower + upper


def transform_kernel(devices, lines, x_ref, wave_ref, twiddle_ref, out_ref):
    bases = [min(tile * TILE, lines - TILE) for tile in range(-(-lines // TILE))]
    for start in range(0, len(bases), 2):
        group = bases[start : start + 2]
        swapped = []
        for base in group:
            swapped += swap_lanes([x_ref[pl.ds(p * lines + base, TILE), :] for p in range(devices)])
        product = jnp.dot(
            jnp.concatenate(swapped, axis=0),
            wave_ref[...],
            precision=lax.Precision.HIGHEST,
            preferred_element_type=jnp.float32,
        )
        for n, base in enumerate(group):
            values = []
            for b in range(devices):
                row = (n * devices + b) * TILE
                re, im = product[row : row + TILE, :LANES], product[row : row + TILE, LANES:]
                if b:
                    cosine, sine = twiddle_ref[0, pl.ds(b, 1), :], twiddle_ref[1, pl.ds(b, 1), :]
                    re, im = re * cosine - im * sine, re * sine + im * cosine
                values.append((re, im))
            for d, value in enumerate(small_dft(values)):
                for c in range(2):
                    out_ref[pl.ds(2 * (d * lines + base) + c, TILE, stride=2), :] = value[c]


def transform(gathered, devices):
    total, local_len = gathered.shape
    lines = total // devices
    wave = jnp.asarray(wave_table(local_len, devices))
    twiddle = jnp.asarray(twiddle_table(local_len, devices))
    return pl.pallas_call(
        functools.partial(transform_kernel, devices, lines),
        out_shape=jax.ShapeDtypeStruct((2 * total, local_len), jnp.float32),
        in_specs=[pl.BlockSpec(memory_space=pltpu.VMEM)] * 3,
        out_specs=pl.BlockSpec(memory_space=pltpu.VMEM),
        compiler_params=pltpu.CompilerParams(vmem_limit_bytes=24 << 20),
        name="transform",
    )(gathered, wave, twiddle)


GROUP = 4
PAIR = 2


def coherence_kernel(rows, levels, spec_ref, out_ref, pitched, norm, cross, sems):
    tiles = -(-levels // TILE)

    def base(tile):
        return jnp.minimum(tile * TILE, levels - TILE)

    pitch = 2 * rows + 1
    for level in range(levels):
        for row in range(0, 2 * rows, TILE):
            pitched[pl.ds(level * pitch + row, TILE), :] = spec_ref[pl.ds(level * 2 * rows + row, TILE), :]

    @pl.loop(0, tiles)
    def _(tile):
        def load(r, c):
            return pitched[pl.ds(base(tile) * pitch + 2 * r + c, TILE, stride=pitch), :]

        res = [load(r, 0) for r in range(rows)]
        ims = [load(r, 1) for r in range(rows)]
        power = res[0] * res[0] + ims[0] * ims[0]
        for r in range(1, rows):
            power = power + (res[r] * res[r] + ims[r] * ims[r])
        scale = lax.rsqrt(power / rows + EPS) * (1.0 / math.sqrt(rows))
        slot = pl.ds(pl.multiple_of(tile * TILE, TILE), TILE)
        for r in range(rows):
            re, im = res[r] * scale, ims[r] * scale
            norm[0, r, slot, :] = re
            norm[1, r, slot, :] = im
            norm[2, r, slot, :] = re + im
            norm[3, r, slot, :] = re - im

    def products(level, slot, pair, group):
        sums = [[[None] * 3 for _ in pair] for _ in range(group)]
        for r in range(rows):
            right = [
                [norm[q, r, pl.ds(pl.multiple_of(t * TILE, TILE), TILE), :] for q in (0, 2, 3)] for t in pair
            ]
            for g in range(group):
                left = [norm[q, r, pl.ds(slot + g, TILE, stride=0), :] for q in (2, 0, 1)]
                for t in range(len(pair)):
                    for i in range(3):
                        term = left[i] * right[t][i]
                        sums[g][t][i] = term if r == 0 else sums[g][t][i] + term
        for g in range(group):
            for t in range(len(pair)):
                one, two, three = sums[g][t]
                re, im = one - three, one - two
                a, b = level + g, base(pair[t])
                for c, straight, mirrored in ((0, re, re), (1, im, -im)):
                    cross[pl.ds(2 * (a * levels + b) + c, TILE, stride=2), :] = straight
                    cross[pl.ds(2 * (b * levels + a) + c, TILE, stride=2 * levels), :] = mirrored

    def work(tile, level, slot, groups):
        count = tiles - tile
        steps = count // (2 * PAIR)
        left = count - steps * 2 * PAIR

        def pairs(first, number):
            for pair in range(number):
                for group in range(groups):
                    here = [first + pair * PAIR + t for t in range(PAIR)]
                    products(level + group * GROUP, slot + group * GROUP, here, GROUP)

        @pl.loop(0, steps)
        def _(step):
            pairs(tile + step * 2 * PAIR, 2)

        def end(number):
            pairs(tile + steps * 2 * PAIR, number // PAIR)
            if number % PAIR:
                products(level, slot, [tiles - 1], groups * GROUP)

        for number in range(1, 2 * PAIR):
            if not isinstance(count, int):
                pl.when(left == number)(functools.partial(end, number))
            elif left == number:
                end(number)

    def copy(tile, count):
        part = pl.ds(pl.multiple_of(tile * (TILE * 2 * levels), TILE), count * 2 * levels)
        return pltpu.make_async_copy(cross.at[part], out_ref.at[part], sems.at[tile])

    last = tiles - 2

    @pl.loop(0, last)
    def _(tile):
        work(tile, tile * TILE, tile * TILE, TILE // GROUP)
        copy(tile, TILE).start()

    work(last, last * TILE, last * TILE, TILE // GROUP)
    rest = levels - (tiles - 1) * TILE
    groups = -(-rest // GROUP)
    work(tiles - 1, levels - groups * GROUP, tiles * TILE - groups * GROUP, groups)
    copy(last, levels - last * TILE).start()

    @pl.loop(0, last)
    def _(tile):
        copy(tile, TILE).wait()

    copy(last, levels - last * TILE).wait()


def coherence(spectra, rows, levels):
    local_len = spectra.shape[1]
    tiles = -(-levels // TILE)
    out_rows = 2 * levels * levels
    return pl.pallas_call(
        functools.partial(coherence_kernel, rows, levels),
        out_shape=jax.ShapeDtypeStruct((out_rows, local_len), jnp.float32),
        in_specs=[pl.BlockSpec(memory_space=pltpu.VMEM)],
        out_specs=pl.BlockSpec(memory_space=pl.ANY),
        scratch_shapes=[
            pltpu.VMEM((levels * (2 * rows + 1), local_len), jnp.float32),
            pltpu.VMEM((4, rows, tiles * TILE, local_len), jnp.float32),
            pltpu.VMEM((out_rows, local_len), jnp.float32),
            pltpu.SemaphoreType.DMA((tiles,)),
        ],
        compiler_params=pltpu.CompilerParams(vmem_limit_bytes=40 << 20),
        name="coherence",
    )(spectra)


def exchange(value, devices):
    rows, local_len = value.shape
    value = value.reshape(devices, rows // (2 * devices), 2, local_len)
    return lax.all_to_all(value, "lon", split_axis=0, concat_axis=0, tiled=True).reshape(rows, local_len)


def local(field):
    devices = lax.axis_size("lon")
    rows, levels, local_len = field.shape
    total = rows * levels
    share = -(-total // (2 * devices)) * 2
    lines = field.transpose(1, 0, 2).reshape(total, local_len)
    lines = jnp.pad(lines, ((0, share * devices - total), (0, 0)))
    spectra = exchange(transform(exchange(lines, devices), devices), devices)
    result = coherence(spectra, rows, levels)
    return result.reshape(levels, levels, 2, local_len).transpose(2, 0, 1, 3)


def solution(mesh):
    in_specs = (P("band", None, "lon"),)
    out_specs = P(None, "band", None, "lon")
    return jax.shard_map(local, mesh=mesh, in_specs=in_specs, out_specs=out_specs, check_vma=False)
```

```python
import functools
import math

import jax
import jax.numpy as jnp
import numpy as np
from jax import lax
from jax.experimental import pallas as pl
from jax.experimental.pallas import tpu as pltpu
from jax.sharding import PartitionSpec as P

EPS = 1e-06
LANES = 128
TILE = 8


def wave_table(local_len, devices):
    lane = np.arange(local_len)
    low, p = lane // devices, lane % devices
    a = (local_len // devices) * p + low
    phase = (a[:, None] * np.arange(local_len)[None, :]) % local_len
    angle = -2.0 * np.pi * phase / local_len
    return np.concatenate([np.cos(angle), np.sin(angle)], axis=1).astype(np.float32)


def twiddle_table(local_len, devices):
    total = local_len * devices
    phase = (np.arange(devices)[:, None] * np.arange(local_len)[None, :]) % total
    angle = -2.0 * np.pi * phase / total
    return np.stack([np.cos(angle), np.sin(angle)]).astype(np.float32)


def swap_lanes(values):
    values = list(values)
    count = len(values)
    lane = lax.broadcasted_iota(jnp.int32, values[0].shape, 1)
    step = 1
    while step < count:
        clear = (lane & step) == 0
        for low in range(count):
            if low & step:
                continue
            first, second = values[low], values[low | step]
            values[low] = jnp.where(clear, first, pltpu.roll(second, step, 1))
            values[low | step] = jnp.where(clear, pltpu.roll(first, LANES - step, 1), second)
        step *= 2
    return values


def small_dft(values):
    count = len(values)
    if count == 1:
        return values
    even, odd = small_dft(values[0::2]), small_dft(values[1::2])
    lower, upper = [], []
    for d in range(count // 2):
        re, im = odd[d]
        if d == 0:
            pass
        elif 4 * d == count:
            re, im = im, -re
        elif 8 * d == count:
            root = math.sqrt(0.5)
            re, im = (re + im) * root, (im - re) * root
        elif 8 * d == 3 * count:
            root = math.sqrt(0.5)
            re, im = (im - re) * root, -(re + im) * root
        else:
            angle = -2.0 * math.pi * d / count
            cosine, sine = math.cos(angle), math.sin(angle)
            re, im = re * cosine - im * sine, re * sine + im * cosine
        lower.append((even[d][0] + re, even[d][1] + im))
        upper.append((even[d][0] - re, even[d][1] - im))
    return lower + upper


def transform_kernel(devices, lines, x_ref, wave_ref, twiddle_ref, out_ref):
    bases = [min(tile * TILE, lines - TILE) for tile in range(-(-lines // TILE))]
    for start in range(0, len(bases), 2):
        group = bases[start : start + 2]
        swapped = []
        for base in group:
            swapped += swap_lanes([x_ref[pl.ds(p * lines + base, TILE), :] for p in range(devices)])
        product = jnp.dot(
            jnp.concatenate(swapped, axis=0),
            wave_ref[...],
            precision=lax.Precision.HIGHEST,
            preferred_element_type=jnp.float32,
        )
        for n, base in enumerate(group):
            values = []
            for b in range(devices):
                row = (n * devices + b) * TILE
                re, im = product[row : row + TILE, :LANES], product[row : row + TILE, LANES:]
                if b:
                    cosine, sine = twiddle_ref[0, pl.ds(b, 1), :], twiddle_ref[1, pl.ds(b, 1), :]
                    re, im = re * cosine - im * sine, re * sine + im * cosine
                values.append((re, im))
            for d, value in enumerate(small_dft(values)):
                for c in range(2):
                    out_ref[pl.ds(2 * (d * lines + base) + c, TILE, stride=2), :] = value[c]


def transform(gathered, devices):
    total, local_len = gathered.shape
    lines = total // devices
    wave = jnp.asarray(wave_table(local_len, devices))
    twiddle = jnp.asarray(twiddle_table(local_len, devices))
    return pl.pallas_call(
        functools.partial(transform_kernel, devices, lines),
        out_shape=jax.ShapeDtypeStruct((2 * total, local_len), jnp.float32),
        in_specs=[pl.BlockSpec(memory_space=pltpu.VMEM)] * 3,
        out_specs=pl.BlockSpec(memory_space=pltpu.VMEM),
        compiler_params=pltpu.CompilerParams(vmem_limit_bytes=24 << 20),
        name="transform",
    )(gathered, wave, twiddle)


GROUP = 4
PAIR = 2
QUANTITIES = 4


def coherence_kernel(rows, levels, spec_ref, out_ref, pitched, norm, cross, sems):
    tiles = -(-levels // TILE)

    def base(tile):
        return jnp.minimum(tile * TILE, levels - TILE)

    pitch = 2 * rows + 1
    for level in range(levels):
        for row in range(0, 2 * rows, TILE):
            pitched[pl.ds(level * pitch + row, TILE), :] = spec_ref[pl.ds(level * 2 * rows + row, TILE), :]

    @pl.loop(0, tiles, unroll=3)
    def _(tile):
        def load(r, c):
            return pitched[pl.ds(base(tile) * pitch + 2 * r + c, TILE, stride=pitch), :]

        res = [load(r, 0) for r in range(rows)]
        ims = [load(r, 1) for r in range(rows)]
        power = res[0] * res[0] + ims[0] * ims[0]
        for r in range(1, rows):
            power = power + (res[r] * res[r] + ims[r] * ims[r])
        scale = lax.rsqrt(power / rows + EPS) * (1.0 / math.sqrt(rows))
        slot = pl.ds(pl.multiple_of(tile * TILE, TILE), TILE)
        for r in range(rows):
            re, im = res[r] * scale, ims[r] * scale
            norm[0, r, slot, :] = re
            norm[1, r, slot, :] = im
            norm[2, r, slot, :] = re + im
            norm[3, r, slot, :] = re - im

    def products(level, slot, pair, group):
        sums = [[[None] * 3 for _ in pair] for _ in range(group)]
        for r in range(rows):
            right = [
                [norm[q, r, pl.ds(pl.multiple_of(t * TILE, TILE), TILE), :] for q in (0, 2, 3)] for t in pair
            ]
            for g in range(group):
                left = [norm[q, r, pl.ds(slot + g, TILE, stride=0), :] for q in (2, 0, 1)]
                for t in range(len(pair)):
                    for i in range(3):
                        term = left[i] * right[t][i]
                        sums[g][t][i] = term if r == 0 else sums[g][t][i] + term
        for g in range(group):
            for t in range(len(pair)):
                one, two, three = sums[g][t]
                re, im = one - three, one - two
                a, b = level + g, base(pair[t])
                for c, straight, mirrored in ((0, re, re), (1, im, -im)):
                    cross[pl.ds(2 * (a * levels + b) + c, TILE, stride=2), :] = straight
                    cross[pl.ds(2 * (b * levels + a) + c, TILE, stride=2 * levels), :] = mirrored

    def diagonal(level, tile):
        slot = pl.ds(pl.multiple_of(tile * TILE, TILE), TILE)
        power = None
        sums = [[None] * 3 for _ in range(TILE // 2)]
        for r in range(rows):
            re, im, plus, minus = [norm[q, r, slot, :] for q in range(QUANTITIES)]
            term = re * re + im * im
            power = term if r == 0 else power + term
            for shift in range(1, TILE // 2 + 1):
                for i, (left, right) in enumerate(((plus, re), (re, plus), (im, minus))):
                    term = pltpu.roll(left, TILE - shift, 0) * right
                    sums[shift - 1][i] = term if r == 0 else sums[shift - 1][i] + term
        stride = 2 * (levels + 1)
        start = 2 * level * (levels + 1)
        cross[pl.ds(start, TILE, stride=stride), :] = power
        cross[pl.ds(start + 1, TILE, stride=stride), :] = jnp.zeros_like(power)
        for shift in range(1, TILE // 2 + 1):
            one, two, three = sums[shift - 1]
            re, im = one - three, one - two
            kept = TILE - shift
            for c, straight, mirrored in ((0, re, re), (1, im, -im)):
                low = 2 * shift * levels + c
                cross[pl.ds(start + low, kept, stride=stride), :] = straight[:kept]
                high = kept * stride - 2 * kept * levels + c
                cross[pl.ds(start + high, shift, stride=stride), :] = straight[kept:]
                if shift < TILE // 2:
                    cross[pl.ds(start + 2 * shift + c, kept, stride=stride), :] = mirrored[:kept]
                    cross[pl.ds(start + 2 * kept * levels + c, shift, stride=stride), :] = mirrored[kept:]

    def work(tile, level, slot, groups):
        diagonal(level, tile)
        tile = tile + 1
        count = tiles - tile
        steps = count // (2 * PAIR)
        left = count - steps * 2 * PAIR

        def pairs(first, number):
            for pair in range(number):
                for group in range(groups):
                    here = [first + pair * PAIR + t for t in range(PAIR)]
                    products(level + group * GROUP, slot + group * GROUP, here, GROUP)

        @pl.loop(0, steps)
        def _(step):
            pairs(tile + step * 2 * PAIR, 2)

        def end(number):
            pairs(tile + steps * 2 * PAIR, number // PAIR)
            if number % PAIR:
                products(level, slot, [tiles - 1], groups * GROUP)

        for number in range(1, 2 * PAIR):
            if not isinstance(count, int):
                pl.when(left == number)(functools.partial(end, number))
            elif left == number:
                end(number)

    def copy(tile, count):
        part = pl.ds(pl.multiple_of(tile * (TILE * 2 * levels), TILE), count * 2 * levels)
        return pltpu.make_async_copy(cross.at[part], out_ref.at[part], sems.at[tile])

    last = tiles - 2

    @pl.loop(0, last)
    def _(tile):
        work(tile, tile * TILE, tile * TILE, TILE // GROUP)
        copy(tile, TILE).start()

    work(last, last * TILE, last * TILE, TILE // GROUP)
    diagonal(levels - TILE, tiles - 1)
    copy(last, levels - last * TILE).start()

    @pl.loop(0, last)
    def _(tile):
        copy(tile, TILE).wait()

    copy(last, levels - last * TILE).wait()


def coherence(spectra, rows, levels):
    local_len = spectra.shape[1]
    tiles = -(-levels // TILE)
    out_rows = 2 * levels * levels
    return pl.pallas_call(
        functools.partial(coherence_kernel, rows, levels),
        out_shape=jax.ShapeDtypeStruct((out_rows, local_len), jnp.float32),
        in_specs=[pl.BlockSpec(memory_space=pltpu.VMEM)],
        out_specs=pl.BlockSpec(memory_space=pl.ANY),
        scratch_shapes=[
            pltpu.VMEM((levels * (2 * rows + 1), local_len), jnp.float32),
            pltpu.VMEM((4, rows, tiles * TILE, local_len), jnp.float32),
            pltpu.VMEM((out_rows, local_len), jnp.float32),
            pltpu.SemaphoreType.DMA((tiles,)),
        ],
        compiler_params=pltpu.CompilerParams(vmem_limit_bytes=40 << 20),
        name="coherence",
    )(spectra)


def exchange(value, devices):
    rows, local_len = value.shape
    value = value.reshape(devices, rows // (2 * devices), 2, local_len)
    return lax.all_to_all(value, "lon", split_axis=0, concat_axis=0, tiled=True).reshape(rows, local_len)


def local(field):
    devices = lax.axis_size("lon")
    rows, levels, local_len = field.shape
    total = rows * levels
    share = -(-total // (2 * devices)) * 2
    lines = field.transpose(1, 0, 2).reshape(total, local_len)
    lines = jnp.pad(lines, ((0, share * devices - total), (0, 0)))
    spectra = exchange(transform(exchange(lines, devices), devices), devices)
    result = coherence(spectra, rows, levels)
    return result.reshape(levels, levels, 2, local_len).transpose(2, 0, 1, 3)


def solution(mesh):
    in_specs = (P("band", None, "lon"),)
    out_specs = P(None, "band", None, "lon")
    return jax.shard_map(local, mesh=mesh, in_specs=in_specs, out_specs=out_specs, check_vma=False)
```

```python
import functools
import math

import jax
import jax.numpy as jnp
import numpy as np
from jax import lax
from jax.experimental import pallas as pl
from jax.experimental.pallas import tpu as pltpu
from jax.sharding import PartitionSpec as P

EPS = 1e-06
LANES = 128
TILE = 8


def wave_table(local_len, devices):
    lane = np.arange(local_len)
    low, p = lane // devices, lane % devices
    a = (local_len // devices) * p + low
    phase = (a[:, None] * np.arange(local_len)[None, :]) % local_len
    angle = -2.0 * np.pi * phase / local_len
    return np.concatenate([np.cos(angle), np.sin(angle)], axis=1).astype(np.float32)


def twiddle_table(local_len, devices):
    total = local_len * devices
    phase = (np.arange(devices)[:, None] * np.arange(local_len)[None, :]) % total
    angle = -2.0 * np.pi * phase / total
    return np.stack([np.cos(angle), np.sin(angle)]).astype(np.float32)


def swap_lanes(values):
    values = list(values)
    count = len(values)
    lane = lax.broadcasted_iota(jnp.int32, values[0].shape, 1)
    step = 1
    while step < count:
        clear = (lane & step) == 0
        for low in range(count):
            if low & step:
                continue
            first, second = values[low], values[low | step]
            values[low] = jnp.where(clear, first, pltpu.roll(second, step, 1))
            values[low | step] = jnp.where(clear, pltpu.roll(first, LANES - step, 1), second)
        step *= 2
    return values


def small_dft(values):
    count = len(values)
    if count == 1:
        return values
    even, odd = small_dft(values[0::2]), small_dft(values[1::2])
    lower, upper = [], []
    for d in range(count // 2):
        re, im = odd[d]
        if d == 0:
            pass
        elif 4 * d == count:
            re, im = im, -re
        elif 8 * d == count:
            root = math.sqrt(0.5)
            re, im = (re + im) * root, (im - re) * root
        elif 8 * d == 3 * count:
            root = math.sqrt(0.5)
            re, im = (im - re) * root, -(re + im) * root
        else:
            angle = -2.0 * math.pi * d / count
            cosine, sine = math.cos(angle), math.sin(angle)
            re, im = re * cosine - im * sine, re * sine + im * cosine
        lower.append((even[d][0] + re, even[d][1] + im))
        upper.append((even[d][0] - re, even[d][1] - im))
    return lower + upper


def transform_kernel(devices, lines, x_ref, wave_ref, twiddle_ref, out_ref):
    bases = [min(tile * TILE, lines - TILE) for tile in range(-(-lines // TILE))]
    for start in range(0, len(bases), 2):
        group = bases[start : start + 2]
        swapped = []
        for base in group:
            swapped += swap_lanes([x_ref[pl.ds(p * lines + base, TILE), :] for p in range(devices)])
        product = jnp.dot(
            jnp.concatenate(swapped, axis=0),
            wave_ref[...],
            precision=lax.Precision.HIGHEST,
            preferred_element_type=jnp.float32,
        )
        for n, base in enumerate(group):
            values = []
            for b in range(devices):
                row = (n * devices + b) * TILE
                re, im = product[row : row + TILE, :LANES], product[row : row + TILE, LANES:]
                if b:
                    cosine, sine = twiddle_ref[0, pl.ds(b, 1), :], twiddle_ref[1, pl.ds(b, 1), :]
                    re, im = re * cosine - im * sine, re * sine + im * cosine
                values.append((re, im))
            for d, value in enumerate(small_dft(values)):
                for c in range(2):
                    out_ref[pl.ds(2 * (d * lines + base) + c, TILE, stride=2), :] = value[c]


def transform(gathered, devices):
    total, local_len = gathered.shape
    lines = total // devices
    wave = jnp.asarray(wave_table(local_len, devices))
    twiddle = jnp.asarray(twiddle_table(local_len, devices))
    return pl.pallas_call(
        functools.partial(transform_kernel, devices, lines),
        out_shape=jax.ShapeDtypeStruct((2 * total, local_len), jnp.float32),
        in_specs=[pl.BlockSpec(memory_space=pltpu.VMEM)] * 3,
        out_specs=pl.BlockSpec(memory_space=pltpu.VMEM),
        compiler_params=pltpu.CompilerParams(vmem_limit_bytes=24 << 20),
        name="transform",
    )(gathered, wave, twiddle)


GROUP = 4
PAIR = 2
QUANTITIES = 4


def coherence_kernel(rows, levels, spec_ref, out_ref, pitched, norm, cross, sems):
    tiles, whole = -(-levels // TILE), levels // TILE

    def base(tile):
        return jnp.minimum(tile * TILE, levels - TILE)

    pitch = 2 * rows + 1
    for level in range(levels):
        for row in range(0, 2 * rows, TILE):
            pitched[pl.ds(level * pitch + row, TILE), :] = spec_ref[pl.ds(level * 2 * rows + row, TILE), :]

    @pl.loop(0, tiles, unroll=3)
    def _(tile):
        def load(r, c):
            return pitched[pl.ds(base(tile) * pitch + 2 * r + c, TILE, stride=pitch), :]

        res = [load(r, 0) for r in range(rows)]
        ims = [load(r, 1) for r in range(rows)]
        power = res[0] * res[0] + ims[0] * ims[0]
        for r in range(1, rows):
            power = power + (res[r] * res[r] + ims[r] * ims[r])
        scale = lax.rsqrt(power / rows + EPS) * (1.0 / math.sqrt(rows))
        slot = pl.ds(pl.multiple_of(tile * TILE, TILE), TILE)
        for r in range(rows):
            re, im = res[r] * scale, ims[r] * scale
            norm[0, r, slot, :] = re
            norm[1, r, slot, :] = im
            norm[2, r, slot, :] = re + im
            norm[3, r, slot, :] = re - im

    def products(level, slot, pair, group):
        sums = [[[None] * 3 for _ in pair] for _ in range(group)]
        for r in range(rows):
            right = [
                [norm[q, r, pl.ds(pl.multiple_of(t * TILE, TILE), TILE), :] for q in (0, 2, 3)] for t in pair
            ]
            for g in range(group):
                left = [norm[q, r, pl.ds(slot + g, TILE, stride=0), :] for q in (2, 0, 1)]
                for t in range(len(pair)):
                    for i in range(3):
                        term = left[i] * right[t][i]
                        sums[g][t][i] = term if r == 0 else sums[g][t][i] + term
        for g in range(group):
            for t in range(len(pair)):
                one, two, three = sums[g][t]
                re, im = one - three, one - two
                a, b = level + g, base(pair[t])
                for c, straight, mirrored in ((0, re, re), (1, im, -im)):
                    cross[pl.ds(2 * (a * levels + b) + c, TILE, stride=2), :] = straight
                    cross[pl.ds(2 * (b * levels + a) + c, TILE, stride=2 * levels), :] = mirrored

    def diagonal(level, tile):
        slot = pl.ds(pl.multiple_of(tile * TILE, TILE), TILE)
        power = None
        sums = [[None] * 3 for _ in range(TILE // 2)]
        for r in range(rows):
            re, im, plus, minus = [norm[q, r, slot, :] for q in range(QUANTITIES)]
            term = re * re + im * im
            power = term if r == 0 else power + term
            for shift in range(1, TILE // 2 + 1):
                for i, (left, right) in enumerate(((plus, re), (re, plus), (im, minus))):
                    term = pltpu.roll(left, TILE - shift, 0) * right
                    sums[shift - 1][i] = term if r == 0 else sums[shift - 1][i] + term
        stride = 2 * (levels + 1)
        start = 2 * level * (levels + 1)
        cross[pl.ds(start, TILE, stride=stride), :] = power
        cross[pl.ds(start + 1, TILE, stride=stride), :] = jnp.zeros_like(power)
        for shift in range(1, TILE // 2 + 1):
            one, two, three = sums[shift - 1]
            re, im = one - three, one - two
            kept = TILE - shift
            for c, straight, mirrored in ((0, re, re), (1, im, -im)):
                low = 2 * shift * levels + c
                cross[pl.ds(start + low, kept, stride=stride), :] = straight[:kept]
                high = kept * stride - 2 * kept * levels + c
                cross[pl.ds(start + high, shift, stride=stride), :] = straight[kept:]
                if shift < TILE // 2:
                    cross[pl.ds(start + 2 * shift + c, kept, stride=stride), :] = mirrored[:kept]
                    cross[pl.ds(start + 2 * kept * levels + c, shift, stride=stride), :] = mirrored[kept:]

    def work(tile, level, slot, groups):
        diagonal(level, tile)
        tile = tile + 1
        count = whole - tile
        steps = count // (2 * PAIR)
        left = count - steps * 2 * PAIR

        def pairs(first, number):
            for pair in range(number):
                for group in range(groups):
                    here = [first + pair * PAIR + t for t in range(PAIR)]
                    products(level + group * GROUP, slot + group * GROUP, here, GROUP)

        @pl.loop(0, steps)
        def _(step):
            pairs(tile + step * 2 * PAIR, 2)

        def end(number):
            pairs(tile + steps * 2 * PAIR, number // PAIR)
            if number % PAIR:
                products(level, slot, [whole - 1], groups * GROUP)

        for number in range(1, 2 * PAIR):
            if not isinstance(count, int):
                pl.when(left == number)(functools.partial(end, number))
            elif left == number:
                end(number)

    def copy(tile, count):
        part = pl.ds(pl.multiple_of(tile * (TILE * 2 * levels), TILE), count * 2 * levels)
        return pltpu.make_async_copy(cross.at[part], out_ref.at[part], sems.at[tile])

    last = tiles - 2
    rest = levels % TILE
    for tile in range(0, whole if rest else 0, 2 * PAIR):
        pair = list(range(tile, min(tile + 2 * PAIR, whole)))
        for group in range(0, rest, PAIR):
            products(levels - rest + group, tiles * TILE - rest + group, pair, min(PAIR, rest - group))

    @pl.loop(0, last)
    def _(tile):
        work(tile, tile * TILE, tile * TILE, TILE // GROUP)
        copy(tile, TILE).start()

    work(last, last * TILE, last * TILE, TILE // GROUP)
    diagonal(levels - TILE, tiles - 1)
    copy(last, levels - last * TILE).start()

    @pl.loop(0, last)
    def _(tile):
        copy(tile, TILE).wait()

    copy(last, levels - last * TILE).wait()


def coherence(spectra, rows, levels):
    local_len = spectra.shape[1]
    tiles = -(-levels // TILE)
    out_rows = 2 * levels * levels
    return pl.pallas_call(
        functools.partial(coherence_kernel, rows, levels),
        out_shape=jax.ShapeDtypeStruct((out_rows, local_len), jnp.float32),
        in_specs=[pl.BlockSpec(memory_space=pltpu.VMEM)],
        out_specs=pl.BlockSpec(memory_space=pl.ANY),
        scratch_shapes=[
            pltpu.VMEM((levels * (2 * rows + 1), local_len), jnp.float32),
            pltpu.VMEM((4, rows, tiles * TILE, local_len), jnp.float32),
            pltpu.VMEM((out_rows, local_len), jnp.float32),
            pltpu.SemaphoreType.DMA((tiles,)),
        ],
        compiler_params=pltpu.CompilerParams(vmem_limit_bytes=40 << 20),
        name="coherence",
    )(spectra)


def exchange(value, devices):
    rows, local_len = value.shape
    value = value.reshape(devices, rows // (2 * devices), 2, local_len)
    return lax.all_to_all(value, "lon", split_axis=0, concat_axis=0, tiled=True).reshape(rows, local_len)


def local(field):
    devices = lax.axis_size("lon")
    rows, levels, local_len = field.shape
    total = rows * levels
    share = -(-total // (2 * devices)) * 2
    lines = field.transpose(1, 0, 2).reshape(total, local_len)
    lines = jnp.pad(lines, ((0, share * devices - total), (0, 0)))
    spectra = exchange(transform(exchange(lines, devices), devices), devices)
    result = coherence(spectra, rows, levels)
    return result.reshape(levels, levels, 2, local_len).transpose(2, 0, 1, 3)


def solution(mesh):
    in_specs = (P("band", None, "lon"),)
    out_specs = P(None, "band", None, "lon")
    return jax.shard_map(local, mesh=mesh, in_specs=in_specs, out_specs=out_specs, check_vma=False)
```

```python
import functools
import math

import jax
import jax.numpy as jnp
import numpy as np
from jax import lax
from jax.experimental import pallas as pl
from jax.experimental.pallas import tpu as pltpu
from jax.sharding import PartitionSpec as P

EPS = 1e-06
LANES = 128
TILE = 8


def wave_table(local_len, devices):
    lane = np.arange(local_len)
    low, p = lane // devices, lane % devices
    a = (local_len // devices) * p + low
    phase = (a[:, None] * np.arange(local_len)[None, :]) % local_len
    angle = -2.0 * np.pi * phase / local_len
    return np.concatenate([np.cos(angle), np.sin(angle)], axis=1).astype(np.float32)


def twiddle_table(local_len, devices):
    total = local_len * devices
    phase = (np.arange(devices)[:, None] * np.arange(local_len)[None, :]) % total
    angle = -2.0 * np.pi * phase / total
    return np.stack([np.cos(angle), np.sin(angle)]).astype(np.float32)


def swap_lanes(values):
    values = list(values)
    count = len(values)
    lane = lax.broadcasted_iota(jnp.int32, values[0].shape, 1)
    step = 1
    while step < count:
        clear = (lane & step) == 0
        for low in range(count):
            if low & step:
                continue
            first, second = values[low], values[low | step]
            values[low] = jnp.where(clear, first, pltpu.roll(second, step, 1))
            values[low | step] = jnp.where(clear, pltpu.roll(first, LANES - step, 1), second)
        step *= 2
    return values


def small_dft(values):
    count = len(values)
    if count == 1:
        return values
    even, odd = small_dft(values[0::2]), small_dft(values[1::2])
    lower, upper = [], []
    for d in range(count // 2):
        re, im = odd[d]
        if d == 0:
            pass
        elif 4 * d == count:
            re, im = im, -re
        elif 8 * d == count:
            root = math.sqrt(0.5)
            re, im = (re + im) * root, (im - re) * root
        elif 8 * d == 3 * count:
            root = math.sqrt(0.5)
            re, im = (im - re) * root, -(re + im) * root
        else:
            angle = -2.0 * math.pi * d / count
            cosine, sine = math.cos(angle), math.sin(angle)
            re, im = re * cosine - im * sine, re * sine + im * cosine
        lower.append((even[d][0] + re, even[d][1] + im))
        upper.append((even[d][0] - re, even[d][1] - im))
    return lower + upper


def transform_kernel(devices, lines, x_ref, wave_ref, twiddle_ref, out_ref):
    bases = [min(tile * TILE, lines - TILE) for tile in range(-(-lines // TILE))]
    for start in range(0, len(bases), 3):
        group = bases[start : start + 3]
        swapped = []
        for base in group:
            swapped += swap_lanes([x_ref[pl.ds(p * lines + base, TILE), :] for p in range(devices)])
        product = jnp.dot(
            jnp.concatenate(swapped, axis=0),
            wave_ref[...],
            precision=lax.Precision.HIGHEST,
            preferred_element_type=jnp.float32,
        )
        for n, base in enumerate(group):
            values = []
            for b in range(devices):
                row = (n * devices + b) * TILE
                re, im = product[row : row + TILE, :LANES], product[row : row + TILE, LANES:]
                if b:
                    cosine, sine = twiddle_ref[0, pl.ds(b, 1), :], twiddle_ref[1, pl.ds(b, 1), :]
                    re, im = re * cosine - im * sine, re * sine + im * cosine
                values.append((re, im))
            for d, value in enumerate(small_dft(values)):
                for c in range(2):
                    out_ref[pl.ds(2 * (d * lines + base) + c, TILE, stride=2), :] = value[c]


def transform(gathered, devices):
    total, local_len = gathered.shape
    lines = total // devices
    wave = jnp.asarray(wave_table(local_len, devices))
    twiddle = jnp.asarray(twiddle_table(local_len, devices))
    return pl.pallas_call(
        functools.partial(transform_kernel, devices, lines),
        out_shape=jax.ShapeDtypeStruct((2 * total, local_len), jnp.float32),
        in_specs=[pl.BlockSpec(memory_space=pltpu.VMEM)] * 3,
        out_specs=pl.BlockSpec(memory_space=pltpu.VMEM),
        compiler_params=pltpu.CompilerParams(vmem_limit_bytes=24 << 20),
        name="transform",
    )(gathered, wave, twiddle)


GROUP = 4
PAIR = 2
QUANTITIES = 4


def coherence_kernel(rows, levels, spec_ref, out_ref, pitched, norm, cross, sems):
    tiles, whole = -(-levels // TILE), levels // TILE

    def base(tile):
        return jnp.minimum(tile * TILE, levels - TILE)

    pitch = 2 * rows + 1
    for level in range(levels):
        for row in range(0, 2 * rows, TILE):
            pitched[pl.ds(level * pitch + row, TILE), :] = spec_ref[pl.ds(level * 2 * rows + row, TILE), :]

    @pl.loop(0, tiles, unroll=4)
    def _(tile):
        def load(r, c):
            return pitched[pl.ds(base(tile) * pitch + 2 * r + c, TILE, stride=pitch), :]

        res = [load(r, 0) for r in range(rows)]
        ims = [load(r, 1) for r in range(rows)]
        power = res[0] * res[0] + ims[0] * ims[0]
        for r in range(1, rows):
            power = power + (res[r] * res[r] + ims[r] * ims[r])
        scale = lax.rsqrt(power / rows + EPS) * (1.0 / math.sqrt(rows))
        slot = pl.ds(pl.multiple_of(tile * TILE, TILE), TILE)
        for r in range(rows):
            re, im = res[r] * scale, ims[r] * scale
            norm[0, r, slot, :] = re
            norm[1, r, slot, :] = im
            norm[2, r, slot, :] = re + im
            norm[3, r, slot, :] = re - im

    def products(level, slot, pair, group):
        sums = [[[None] * 3 for _ in pair] for _ in range(group)]
        for r in range(rows):
            right = [
                [norm[q, r, pl.ds(pl.multiple_of(t * TILE, TILE), TILE), :] for q in (0, 2, 3)] for t in pair
            ]
            for g in range(group):
                left = [norm[q, r, pl.ds(slot + g, TILE, stride=0), :] for q in (2, 0, 1)]
                for t in range(len(pair)):
                    for i in range(3):
                        term = left[i] * right[t][i]
                        sums[g][t][i] = term if r == 0 else sums[g][t][i] + term
        for g in range(group):
            for t in range(len(pair)):
                one, two, three = sums[g][t]
                re, im = one - three, one - two
                a, b = level + g, base(pair[t])
                for c, straight, mirrored in ((0, re, re), (1, im, -im)):
                    cross[pl.ds(2 * (a * levels + b) + c, TILE, stride=2), :] = straight
                    cross[pl.ds(2 * (b * levels + a) + c, TILE, stride=2 * levels), :] = mirrored

    def diagonal(level, tile):
        slot = pl.ds(pl.multiple_of(tile * TILE, TILE), TILE)
        power = None
        sums = [[None] * 3 for _ in range(TILE // 2)]
        for r in range(rows):
            re, im, plus, minus = [norm[q, r, slot, :] for q in range(QUANTITIES)]
            term = re * re + im * im
            power = term if r == 0 else power + term
            for shift in range(1, TILE // 2 + 1):
                for i, (left, right) in enumerate(((plus, re), (re, plus), (im, minus))):
                    term = pltpu.roll(left, TILE - shift, 0) * right
                    sums[shift - 1][i] = term if r == 0 else sums[shift - 1][i] + term
        stride = 2 * (levels + 1)
        start = 2 * level * (levels + 1)
        cross[pl.ds(start, TILE, stride=stride), :] = power
        cross[pl.ds(start + 1, TILE, stride=stride), :] = jnp.zeros_like(power)
        for shift in range(1, TILE // 2 + 1):
            one, two, three = sums[shift - 1]
            re, im = one - three, one - two
            kept = TILE - shift
            for c, straight, mirrored in ((0, re, re), (1, im, -im)):
                low = 2 * shift * levels + c
                cross[pl.ds(start + low, kept, stride=stride), :] = straight[:kept]
                high = kept * stride - 2 * kept * levels + c
                cross[pl.ds(start + high, shift, stride=stride), :] = straight[kept:]
                if shift < TILE // 2:
                    cross[pl.ds(start + 2 * shift + c, kept, stride=stride), :] = mirrored[:kept]
                    cross[pl.ds(start + 2 * kept * levels + c, shift, stride=stride), :] = mirrored[kept:]

    def work(tile, level, slot, groups):
        diagonal(level, tile)
        tile = tile + 1
        count = whole - tile
        steps = count // (2 * PAIR)
        left = count - steps * 2 * PAIR

        def pairs(first, number):
            for pair in range(number):
                for group in range(groups):
                    here = [first + pair * PAIR + t for t in range(PAIR)]
                    products(level + group * GROUP, slot + group * GROUP, here, GROUP)

        @pl.loop(0, steps)
        def _(step):
            pairs(tile + step * 2 * PAIR, 2)

        def end(number):
            pairs(tile + steps * 2 * PAIR, number // PAIR)
            if number % PAIR:
                products(level, slot, [whole - 1], groups * GROUP)

        for number in range(1, 2 * PAIR):
            if not isinstance(count, int):
                pl.when(left == number)(functools.partial(end, number))
            elif left == number:
                end(number)

    def copy(tile, count):
        part = pl.ds(pl.multiple_of(tile * (TILE * 2 * levels), TILE), count * 2 * levels)
        return pltpu.make_async_copy(cross.at[part], out_ref.at[part], sems.at[tile])

    last = tiles - 2
    rest = levels % TILE
    for tile in range(0, whole if rest else 0, 2 * PAIR):
        pair = list(range(tile, min(tile + 2 * PAIR, whole)))
        for group in range(0, rest, PAIR):
            products(levels - rest + group, tiles * TILE - rest + group, pair, min(PAIR, rest - group))

    @pl.loop(0, last)
    def _(tile):
        work(tile, tile * TILE, tile * TILE, TILE // GROUP)
        copy(tile, TILE).start()

    work(last, last * TILE, last * TILE, TILE // GROUP)
    diagonal(levels - TILE, tiles - 1)
    copy(last, levels - last * TILE).start()

    @pl.loop(0, last)
    def _(tile):
        copy(tile, TILE).wait()

    copy(last, levels - last * TILE).wait()


def coherence(spectra, rows, levels):
    local_len = spectra.shape[1]
    tiles = -(-levels // TILE)
    out_rows = 2 * levels * levels
    return pl.pallas_call(
        functools.partial(coherence_kernel, rows, levels),
        out_shape=jax.ShapeDtypeStruct((out_rows, local_len), jnp.float32),
        in_specs=[pl.BlockSpec(memory_space=pltpu.VMEM)],
        out_specs=pl.BlockSpec(memory_space=pl.ANY),
        scratch_shapes=[
            pltpu.VMEM((levels * (2 * rows + 1), local_len), jnp.float32),
            pltpu.VMEM((4, rows, tiles * TILE, local_len), jnp.float32),
            pltpu.VMEM((out_rows, local_len), jnp.float32),
            pltpu.SemaphoreType.DMA((tiles,)),
        ],
        compiler_params=pltpu.CompilerParams(vmem_limit_bytes=40 << 20),
        name="coherence",
    )(spectra)


def exchange(value, devices):
    rows, local_len = value.shape
    value = value.reshape(devices, rows // (2 * devices), 2, local_len)
    return lax.all_to_all(value, "lon", split_axis=0, concat_axis=0, tiled=True).reshape(rows, local_len)


def local(field):
    devices = lax.axis_size("lon")
    rows, levels, local_len = field.shape
    total = rows * levels
    share = -(-total // (2 * devices)) * 2
    lines = field.transpose(1, 0, 2).reshape(total, local_len)
    lines = jnp.pad(lines, ((0, share * devices - total), (0, 0)))
    spectra = exchange(transform(exchange(lines, devices), devices), devices)
    result = coherence(spectra, rows, levels)
    return result.reshape(levels, levels, 2, local_len).transpose(2, 0, 1, 3)


def solution(mesh):
    in_specs = (P("band", None, "lon"),)
    out_specs = P(None, "band", None, "lon")
    return jax.shard_map(local, mesh=mesh, in_specs=in_specs, out_specs=out_specs, check_vma=False)
```
